512 devices in a mesh: grp: 2 (over y_lo), gx: 16 (over x, y_hi), gy: 16 (over z, core).
Axes of the slice: x: 4, y: 8 (y_hi: 4, y_lo: 2; y = y_hi * 2 + y_lo), z: 8, core: 2. Of those that a mesh axis runs over, the one named last changes fastest.
Arguments:
- velocity: float32 [3, 256, 256, 256], P(None, 'gy', 'gx', 'grp'), may hold values from -6 to 6
- stress: float32 [6, 256, 256, 256], P(None, 'gy', 'gx', 'grp'), may hold values from -6 to 6
- buoyancy: float32 [256, 256, 256], P('gy', 'gx', 'grp'), may hold values from 0.5 to 1.5
- lame_lambda: float32 [256, 256, 256], P('gy', 'gx', 'grp'), may hold values from 0.5 to 2
- shear_modulus: float32 [256, 256, 256], P('gy', 'gx', 'grp'), may hold values from 0.3 to 1.5
- pml_flag: int32 [16, 16, 2], P('gy', 'gx', 'grp'), may hold values 0 or 1
- profile_index: int32 [16, 16, 2], P('gy', 'gx', 'grp'), may hold values from 0 to 3
- damping_peak: float32 [4], replicated, may hold values from 0.3 to 1.5
Outputs:
- velocity_next: float32 [3, 256, 256, 256], P(None, 'gy', 'gx', 'grp')
- stress_next: float32 [6, 256, 256, 256], P(None, 'gy', 'gx', 'grp')
- strain_rate: bfloat16 [2, 6, 256, 256, 256], P(None, None, 'gy', 'gx', 'grp')
The draws below stay inside these ranges and needn't reach their ends.
All inputs are finite; a program needn't handle non-finite values. No bound on the sum of `pml_flag` on one device may be relied on, other than what follows from the above.
Results may differ from the reference program's by a relative error of at most 0.002.
Values may be sent and summed in bfloat16 or wider, within the bound.
A program may use at most 64 MiB of HBM per device.

```python
import math
import jax
import jax.numpy as jnp
from jax import lax

CZ = 16
CY = 16
CX = 128
STEPS = 2
PROFILES = 4
NZ = 256
NY = 256
NX = 256
TILES_Z = 16
TILES_Y = 16
TILES_X = 2
N_GRP = 2
N_GX = 16
N_GY = 16


def smooth_wave(key, components):
    mode_count = 4
    key_number = jax.random.fold_in(key, 1)
    key_direction = jax.random.fold_in(key, 2)
    key_phase = jax.random.fold_in(key, 3)
    key_weight = jax.random.fold_in(key, 4)
    frequency = jax.random.uniform(key_number, (3, components, mode_count), jnp.float32, 0.25, 1.0)
    direction = jnp.where(jax.random.bernoulli(key_direction, 0.5, (3, components, mode_count)), 1.0, -1.0)
    frequency = frequency * direction
    phases = jax.random.uniform(key_phase, (components, mode_count), jnp.float32, -math.pi, math.pi)
    weights = jax.random.uniform(key_weight, (components, mode_count), jnp.float32, 0.5, 1.0)
    depth_axis = (jnp.arange(NZ, dtype=jnp.float32) + 0.5) / NZ
    row_axis = (jnp.arange(NY, dtype=jnp.float32) + 0.5) / NY
    column_axis = (jnp.arange(NX, dtype=jnp.float32) + 0.5) / NX
    summed = jnp.zeros((components, NZ, NY, NX), jnp.float32)
    for mode_index in range(mode_count):
        argument = 2.0 * math.pi * (frequency[0, :, mode_index][:, None, None, None] * depth_axis[None, :, None, None] + frequency[1, :, mode_index][:, None, None, None] * row_axis[None, None, :, None] + frequency[2, :, mode_index][:, None, None, None] * column_axis[None, None, None, :]) + phases[:, mode_index][:, None, None, None]
        summed = summed + weights[:, mode_index][:, None, None, None] * jnp.cos(argument)
    return summed / jnp.sum(weights, axis=1)[:, None, None, None]


def drawn_state(key, components, salt):
    base = jax.random.fold_in(key, salt)
    wave = smooth_wave(jax.random.fold_in(base, 11), components)
    rough = jax.random.normal(jax.random.fold_in(base, 12), (components, NZ, NY, NX), jnp.float32)
    return jnp.clip(2.0 * wave + rough, -6.0, 6.0)


def draw_velocity(key, part):
    return drawn_state(key, 3, 101)


def draw_stress(key, part):
    return drawn_state(key, 6, 202)


def touch_ends(array, stream_key, low, top_value):
    place = [jax.random.randint(jax.random.fold_in(stream_key, axis), (), 0, length) for axis, length in enumerate(array.shape)]
    longest = array.shape.index(max(array.shape))
    beside = place[:longest] + [(place[longest] + 1) % array.shape[longest]] + place[longest + 1:]
    return array.at[tuple(place)].set(low).at[tuple(beside)].set(top_value)


def level_of(key, dims, split, smallest, largest):
    level, own = 1.0, jax.random.fold_in(key, 6)
    for axis_at, parts in split:
        heights = jnp.exp(jax.random.uniform(jax.random.fold_in(own, axis_at), (parts,), jnp.float32, smallest / len(split), largest / len(split)))
        level = level * jnp.repeat(heights, dims[axis_at] // parts).reshape([-1 if axis == axis_at else 1 for axis in range(len(dims))])
    return level


def setup_inputs(seed: int = 0) -> dict:
    keys = jax.random.split(jax.random.key(seed), 9)
    return {
        "velocity": draw_velocity(jax.random.fold_in(keys[8], 71), 0),
        "stress": draw_stress(jax.random.fold_in(keys[8], 71), 0),
        "buoyancy": jnp.clip(0.5 + 1.0 * jax.random.uniform(keys[2], (NZ, NY, NX), jnp.float32) ** level_of(keys[2], (NZ, NY, NX), ((0, 16), (1, 16), (2, 2)), -0.2, 0.2), 0.5, 1.5),
        "lame_lambda": jnp.clip(0.5 + 1.5 * jax.random.uniform(keys[3], (NZ, NY, NX), jnp.float32) ** level_of(keys[3], (NZ, NY, NX), ((0, 16), (1, 16), (2, 2)), -0.2, 0.2), 0.5, 2.0),
        "shear_modulus": jnp.clip(0.3 + 1.2 * jax.random.uniform(keys[4], (NZ, NY, NX), jnp.float32) ** level_of(keys[4], (NZ, NY, NX), ((0, 16), (1, 16), (2, 2)), -0.2, 0.2), 0.3, 1.5),
        "pml_flag": touch_ends((jax.random.randint(keys[5], (TILES_Z, TILES_Y, TILES_X), 0, 2) < 1).astype(jnp.int32), jax.random.fold_in(keys[5], 1), 0, 1),
        "profile_index": touch_ends(jax.random.randint(keys[6], (TILES_Z, TILES_Y, TILES_X), 0, PROFILES), jax.random.fold_in(keys[6], 1), 0, PROFILES - 1).astype(jnp.int32),
        "damping_peak": jnp.clip(jnp.exp(jax.random.uniform(keys[7], (PROFILES,), jnp.float32, math.log(0.3), math.log(1.5))), 0.3, 1.5),
    }


COEF_NEAR = 9.0 / 8.0
COEF_FAR = -1.0 / 24.0
TIME_STEP = 0.15


def take_slice(padded, dimension, offset, length):
    return lax.slice_in_dim(padded, offset, offset + length, axis=dimension)


def difference(padded, dimension, forward):
    length = padded.shape[dimension] - 4
    if forward:
        return COEF_NEAR * (take_slice(padded, dimension, 3, length) - take_slice(padded, dimension, 2, length)) + COEF_FAR * (take_slice(padded, dimension, 4, length) - take_slice(padded, dimension, 1, length))
    return COEF_NEAR * (take_slice(padded, dimension, 2, length) - take_slice(padded, dimension, 1, length)) + COEF_FAR * (take_slice(padded, dimension, 3, length) - take_slice(padded, dimension, 0, length))


def pad_plain(grid_field, dimension):
    widths = [(0, 0)] * grid_field.ndim
    widths[dimension] = (2, 2)
    return jnp.pad(grid_field, widths)


def derive(grid_field, dimension, forward):
    if dimension < 2:
        return difference(pad_plain(grid_field, dimension), dimension, forward)
    group_width = NX // N_GRP
    blocks = grid_field.reshape(NZ, NY, N_GRP, group_width)
    rounded = lax.optimization_barrier(blocks.astype(jnp.bfloat16)).astype(jnp.float32)
    zero_rim = jnp.zeros((NZ, NY, 1, 2), jnp.float32)
    lower_rim = jnp.concatenate([zero_rim, rounded[:, :, :-1, -2:]], axis=2)
    upper_rim = jnp.concatenate([rounded[:, :, 1:, :2], zero_rim], axis=2)
    padded = jnp.concatenate([lower_rim, blocks, upper_rim], axis=3)
    return difference(padded, 3, forward).reshape(NZ, NY, NX)


def reference(velocity, stress, buoyancy, lame_lambda, shear_modulus, pml_flag, profile_index, damping_peak):
    table = jnp.arange(PROFILES, dtype=jnp.int32)
    peak_tile = jnp.sum(jnp.where(profile_index[..., None] == table, damping_peak, 0.0), axis=-1)
    tile_rate = pml_flag.astype(jnp.float32) * peak_tile
    depth = (jnp.arange(NZ, dtype=jnp.int32).astype(jnp.float32) + 0.5) / NZ
    ramp = 0.5 + 0.5 * depth * depth
    spread = jnp.broadcast_to(tile_rate[:, None, :, None, :, None], (N_GY, CZ, N_GX, CY, N_GRP, CX)).reshape(NZ, NY, NX)
    damping = spread * ramp[:, None, None]
    retain = 1.0 - 0.5 * TIME_STEP * damping
    divide = 1.0 + 0.5 * TIME_STEP * damping

    def relax(old, increment):
        return (old * retain + TIME_STEP * increment) / divide

    strain_steps = []
    for step_index in range(STEPS):
        stress_xx, stress_xy, stress_xz, stress_yy, stress_yz, stress_zz = stress
        force_x = derive(stress_xx, 2, True) + derive(stress_xy, 1, False) + derive(stress_xz, 0, False)
        force_y = derive(stress_xy, 2, False) + derive(stress_yy, 1, True) + derive(stress_yz, 0, False)
        force_z = derive(stress_xz, 2, False) + derive(stress_yz, 1, False) + derive(stress_zz, 0, True)
        velocity_x = relax(velocity[0], buoyancy * force_x)
        velocity_y = relax(velocity[1], buoyancy * force_y)
        velocity_z = relax(velocity[2], buoyancy * force_z)
        velocity = jnp.stack([velocity_x, velocity_y, velocity_z])
        normal_x = derive(velocity_x, 2, False)
        normal_y = derive(velocity_y, 1, False)
        normal_z = derive(velocity_z, 0, False)
        shear_xy = 0.5 * (derive(velocity_x, 1, True) + derive(velocity_y, 2, True))
        shear_xz = 0.5 * (derive(velocity_x, 0, True) + derive(velocity_z, 2, True))
        shear_yz = 0.5 * (derive(velocity_y, 0, True) + derive(velocity_z, 1, True))
        dilation = normal_x + normal_y + normal_z
        stress = jnp.stack([
            relax(stress_xx, lame_lambda * dilation + 2.0 * shear_modulus * normal_x),
            relax(stress_xy, 2.0 * shear_modulus * shear_xy),
            relax(stress_xz, 2.0 * shear_modulus * shear_xz),
            relax(stress_yy, lame_lambda * dilation + 2.0 * shear_modulus * normal_y),
            relax(stress_yz, 2.0 * shear_modulus * shear_yz),
            relax(stress_zz, lame_lambda * dilation + 2.0 * shear_modulus * normal_z)])
        strain_steps.append(jnp.stack([normal_x, shear_xy, shear_xz, normal_y, shear_yz, normal_z]).astype(jnp.bfloat16))
    return velocity, stress, jnp.stack(strain_steps)
```

```python
import functools

import jax
import jax.numpy as jnp
from jax import lax
from jax.experimental import pallas as pl
from jax.experimental.pallas import tpu as pltpu
from jax.sharding import PartitionSpec as P

MESH = pl.DeviceIdType.MESH
F32 = jnp.float32
BF16 = jnp.bfloat16

STEPS = 2
NEAR = 9.0 / 8.0
RATIO = -1.0 / 27.0
TIME_STEP = 0.15
HALF = 0.5 * TIME_STEP

EDGE = 2

STRESS = {
    "x": ((0, True), (1, False), (2, False)),
    "y": ((1, False), (3, True), (4, False)),
    "z": ((2, False), (4, False), (5, True)),
}
MOTION = {
    "x": ((0, False), (1, True), (2, True)),
    "y": ((0, True), (1, False), (2, True)),
    "z": ((0, True), (1, True), (2, False)),
}


def row_list(kind, upward):
    rows = []
    for slot, (field, forward) in enumerate(kind["y"]):
        rows.append((slot, field, 0))
    for slot, (field, forward) in enumerate(kind["y"]):
        if forward != upward:
            rows.append((slot, field, 1))
    return rows


def kernel(
    depth, rows, lanes,
    vel_hbm, str_hbm, buoy_hbm, lam_hbm, mu_hbm, flag_ref, prof_ref, peak_ref,
    vout_hbm, sout_hbm, eout_hbm,
    s0, s1, v1, v2, sfin, vin, buoy, lam, mu, keep_ref, gain_ref, cross, strain, eout,
    up_send, up_recv, dn_send, dn_recv, grp_send, grp_recv,
    in_sem, out_sem, ysend_sem, yrecv_sem, zsend_sem, zrecv_sem, gsend_sem, grecv_sem,
):
    gx, gy, grp = lax.axis_index("gx"), lax.axis_index("gy"), lax.axis_index("grp")
    n_gx, n_gy = lax.axis_size("gx"), lax.axis_size("gy")
    has_prev_y, has_next_y = gx > 0, gx < n_gx - 1
    has_prev_z, has_next_z = gy > 0, gy < n_gy - 1
    prev_y, next_y = {"gx": gx - 1}, {"gx": gx + 1}
    prev_z, next_z = {"gy": gy - 1}, {"gy": gy + 1}
    other = {"grp": 1 - grp}

    barrier = pltpu.get_barrier_semaphore()

    def greet(device):
        pl.semaphore_signal(barrier, inc=1, device_id=device, device_id_type=MESH)

    greet(other)
    for exists, device in (
        (has_prev_y, prev_y), (has_next_y, next_y), (has_prev_z, prev_z), (has_next_z, next_z),
    ):
        pl.when(exists)(functools.partial(greet, device))

    def planes(ref, field, first, count):
        return ref.at[field, pl.ds(first * rows, count * rows), :]

    def interior(ref, field):
        return planes(ref, field, EDGE, depth)

    def plane(p):
        return pl.ds(pl.multiple_of(p * rows, 8), rows)

    loads = []

    def load(src, dst):
        copy = pltpu.make_async_copy(src, dst, in_sem.at[len(loads)])
        copy.start()
        loads.append(copy)
        return copy

    stress_load = {f: load(str_hbm.at[f], interior(s0, f)) for f in (1, 3, 4, 0, 2, 5)}
    buoy_load = load(buoy_hbm, buoy)
    vel_load = load(vel_hbm, vin)
    lam_load = load(lam_hbm, lam)
    mu_load = load(mu_hbm, mu)

    z_fields = ((s0, (2, 4, 5)), (s1, (2, 4, 5)), (v1, (0, 1, 2)), (v2, (0, 1, 2)))

    def clear_planes(first):
        for ref, fields in z_fields:
            for f in fields:
                ref[f, pl.ds(first * rows, EDGE * rows), :] = jnp.zeros((EDGE * rows, lanes), F32)

    pl.when(jnp.logical_not(has_prev_z))(functools.partial(clear_planes, 0))
    pl.when(jnp.logical_not(has_next_z))(functools.partial(clear_planes, EDGE + depth))

    def clear_recv(ref):
        ref[...] = jnp.zeros_like(ref)

    pl.when(jnp.logical_not(has_prev_y))(functools.partial(clear_recv, up_recv))
    pl.when(jnp.logical_not(has_next_y))(functools.partial(clear_recv, dn_recv))

    choice = prof_ref[0, 0, 0]
    peak = jnp.float32(0.0)
    for i in range(peak_ref.shape[0]):
        peak = peak + jnp.where(choice == i, peak_ref[i], 0.0)
    rate = flag_ref[0, 0, 0].astype(F32) * peak

    def damping_of(shape):
        z = (lax.broadcasted_iota(jnp.int32, shape, 0) + gy * depth).astype(F32)
        q = (z + 0.5) / (depth * n_gy)
        damping = rate * (0.5 + 0.5 * q * q)
        divide = 1.0 + HALF * damping
        return (1.0 - HALF * damping) / divide, (NEAR * TIME_STEP) / divide

    keep_ref[...], gain_ref[...] = damping_of((depth, 8, lanes))

    slot = lax.broadcasted_iota(jnp.int32, (8, lanes), 0)
    lane = lax.broadcasted_iota(jnp.int32, (8, lanes), 1)
    near_lane = jnp.where(grp == 0, lanes - 1, 0)
    far_lane = jnp.where(grp == 0, lanes - 2, 1)

    def picker(k):
        hit = ((slot == 2 * k) & (lane == near_lane)) | ((slot == 2 * k + 1) & (lane == far_lane))
        return jnp.where(hit, 1.0, 0.0).astype(BF16)

    def placer(k, forward):
        near, far = slot == 2 * k, slot == 2 * k + 1
        if forward:
            one = (near & (lane == lanes - 1)) & (grp == 0)
            after = ((near & (lane == lanes - 2)) | (far & (lane == lanes - 1))) & (grp == 0)
            before = (near & (lane == 0)) & (grp == 1)
            whole = jnp.where(one, 1.0, 0.0)
        else:
            one = (near & (lane == 0)) & (grp == 1)
            after = (near & (lane == lanes - 1)) & (grp == 0)
            before = ((near & (lane == 1)) | (far & (lane == 0))) & (grp == 1)
            whole = jnp.where(one, -1.0, 0.0)
        part = jnp.where(after, RATIO, jnp.where(before, -RATIO, 0.0))
        high = part.astype(BF16)
        low = (part - high.astype(F32)).astype(BF16)
        return jnp.concatenate([whole.astype(BF16) + high, low], axis=0)

    def send_columns(e, kind, ref):
        total = None
        for k, (f, _) in enumerate(kind["x"]):
            cells = ref[f, pl.ds(EDGE * rows, depth * rows), :]
            term = lax.dot_general(
                picker(k), cells.astype(BF16), (((1,), (1,)), ((), ())), preferred_element_type=F32
            )
            total = term if total is None else total + term
        grp_send[e] = total

    def columns_copy(e):
        return pltpu.make_async_remote_copy(
            src_ref=grp_send.at[e], dst_ref=grp_recv.at[e], send_sem=gsend_sem.at[e], recv_sem=grecv_sem.at[e],
            device_id=other, device_id_type=MESH,
        )

    def place_columns(e, kind):
        got = grp_recv[e].astype(BF16)
        pair = jnp.concatenate([got, got], axis=0)
        for k, (_, forward) in enumerate(kind["x"]):
            cross[k] = lax.dot_general(
                pair, placer(k, forward), (((0,), (0,)), ((), ())), preferred_element_type=F32
            )

    def row_at(ref, field, y):
        return ref.at[field, pl.ds(EDGE * rows + y, depth, stride=rows), :]

    def cell_row(ref, y):
        return ref.at[pl.ds(y, depth, stride=rows), :]

    def rows_copy(e, upward, count):
        src, dst = (up_send, up_recv) if upward else (dn_send, dn_recv)
        way = 0 if upward else 1
        return pltpu.make_async_remote_copy(
            src_ref=src.at[e, pl.ds(0, count)], dst_ref=dst.at[e, pl.ds(0, count)],
            send_sem=ysend_sem.at[e, way], recv_sem=yrecv_sem.at[e, way],
            device_id=next_y if upward else prev_y, device_id_type=MESH,
        )

    def planes_copies(e, kind, ref, upward):
        way = 0 if upward else 1
        copies = []
        for k, (f, forward) in enumerate(kind["z"]):
            count = 1 if forward == upward else 2
            first = EDGE + depth - count if upward else EDGE
            target = EDGE - count if upward else EDGE + depth
            copies.append(pltpu.make_async_remote_copy(
                src_ref=planes(ref, f, first, count),
                dst_ref=planes(ref, f, target, count),
                send_sem=zsend_sem.at[e, way, k], recv_sem=zrecv_sem.at[e, way, k],
                device_id=next_z if upward else prev_z, device_id_type=MESH,
            ))
        return copies

    kinds = (STRESS, MOTION) * STEPS
    refs = (s0, v1, s1, v2)

    def start_rows(e):
        kind = kinds[e]
        pl.when(has_next_y)(lambda: rows_copy(e, True, len(row_list(kind, True))).start())
        pl.when(has_prev_y)(lambda: rows_copy(e, False, len(row_list(kind, False))).start())

    def start_planes(e):
        for exists, upward in ((has_next_z, True), (has_prev_z, False)):
            @pl.when(exists)
            def _():
                for copy in planes_copies(e, kinds[e], refs[e], upward):
                    copy.start()

    def wait_planes(e):
        for exists, upward in ((has_prev_z, True), (has_next_z, False)):
            @pl.when(exists)
            def _():
                for copy in planes_copies(e, kinds[e], refs[e], upward):
                    copy.wait_recv()

    def wait_rows(e):
        kind = kinds[e]
        pl.when(has_prev_y)(lambda: rows_copy(e, True, len(row_list(kind, True))).wait_recv())
        pl.when(has_next_y)(lambda: rows_copy(e, False, len(row_list(kind, False))).wait_recv())

    def row_terms(e):
        kind = kinds[e]
        before, after = {}, {}
        for place, (k, _, far) in enumerate(row_list(kind, True)):
            before[k, far] = up_recv[e, place]
        for place, (k, _, far) in enumerate(row_list(kind, False)):
            after[k, far] = dn_recv[e, place]
        terms = []
        for k, (_, forward) in enumerate(kind["y"]):
            if forward:
                terms.append({
                    0: -RATIO * before[k, 0],
                    rows - 1: after[k, 0] + RATIO * after[k, 1],
                    rows - 2: RATIO * after[k, 0],
                })
            else:
                terms.append({
                    0: -before[k, 0] - RATIO * before[k, 1],
                    1: -RATIO * before[k, 0],
                    rows - 1: RATIO * after[k, 0],
                })
        return terms

    def fill_rows(e, values):
        kind, ref = kinds[e], refs[e]

        def value(field, y):
            got = values.get((field, y))
            return row_at(ref, field, y)[...] if got is None else got

        for place, (_, field, far) in enumerate(row_list(kind, True)):
            up_send[e, place] = value(field, rows - 1 - far)
        for place, (_, field, far) in enumerate(row_list(kind, False)):
            dn_send[e, place] = value(field, far)

    lane_id = lax.broadcasted_iota(jnp.int32, (rows, lanes), 1)
    row_id = lax.broadcasted_iota(jnp.int32, (rows, lanes), 0)

    def along_x(ref, field, p, forward):
        cells = ref[field, plane(p), :]
        one_back = jnp.where(lane_id >= 1, pltpu.roll(cells, 1, 1), 0.0)
        one_on = jnp.where(lane_id < lanes - 1, pltpu.roll(cells, lanes - 1, 1), 0.0)
        if forward:
            two_on = jnp.where(lane_id < lanes - 2, pltpu.roll(cells, lanes - 2, 1), 0.0)
            return one_on - cells, two_on - one_back
        two_back = jnp.where(lane_id >= 2, pltpu.roll(cells, 2, 1), 0.0)
        return cells - one_back, one_on - two_back

    def along_y(ref, field, p, forward):
        start = pl.multiple_of(p * rows, 8)

        def at(d):
            cells = ref[field, pl.ds(start + d, rows), :]
            if d == 0:
                return cells
            inside = row_id >= -d if d < 0 else row_id < rows - d
            return jnp.where(inside, cells, 0.0)

        if forward:
            return at(1) - at(0), at(2) - at(-1)
        return at(0) - at(-1), at(1) - at(-2)

    def along_z(ref, field, p, forward):
        at = lambda d: ref[field, plane(p + d), :]
        if forward:
            return at(1) - at(0), at(2) - at(-1)
        return at(0) - at(-1), at(1) - at(-2)

    def per_plane(ref, z):
        block = ref[z]
        return jnp.concatenate([block] * (rows // 8), axis=0)

    def inner(ref, z):
        return ref[plane(z), :]

    def joined(parts, extra):
        near = functools.reduce(lambda a, b: a + b, [n for n, _ in parts])
        far = functools.reduce(lambda a, b: a + b, [f for _, f in parts])
        total = near + RATIO * far
        return total if extra is None else total + extra

    def motion_plane(src, old, new, z):
        p = z + EDGE
        keep, weight = per_plane(keep_ref, z), inner(buoy, z)
        cases = (
            ((along_x, 0, True), (along_y, 1, False), (along_z, 2, False)),
            ((along_x, 1, False), (along_y, 3, True), (along_z, 4, False)),
            ((along_x, 2, False), (along_y, 4, False), (along_z, 5, True)),
        )
        for k, case in enumerate(cases):
            force = joined([way(src, f, p, fwd) for way, f, fwd in case], cross[k, plane(z), :])
            new[k, plane(p), :] = keep * old(k, z) + weight * force

    def tensor_plane(src, old, store, step, z):
        p = z + EDGE
        keep, lam_z, mu_z = per_plane(keep_ref, z), inner(lam, z), inner(mu, z)
        xx = joined([along_x(src, 0, p, False)], cross[0, plane(z), :])
        yy = joined([along_y(src, 1, p, False)], None)
        zz = joined([along_z(src, 2, p, False)], None)
        xy = joined([along_y(src, 0, p, True), along_x(src, 1, p, True)], cross[1, plane(z), :])
        xz = joined([along_z(src, 0, p, True), along_x(src, 2, p, True)], cross[2, plane(z), :])
        yz = joined([along_z(src, 1, p, True), along_y(src, 2, p, True)], None)
        spread = lam_z * (xx + yy + zz)
        twice = mu_z + mu_z
        store(0, z, keep * old(0, z) + (spread + twice * xx))
        store(1, z, keep * old(1, z) + mu_z * xy)
        store(2, z, keep * old(2, z) + mu_z * xz)
        store(3, z, keep * old(3, z) + (spread + twice * yy))
        store(4, z, keep * old(4, z) + mu_z * yz)
        store(5, z, keep * old(5, z) + (spread + twice * zz))
        strain[0, plane(z), :] = xy
        strain[1, plane(z), :] = yy
        strain[2, plane(z), :] = yz
        eout[6 * step + 0, plane(z), :] = (NEAR * xx).astype(BF16)
        eout[6 * step + 2, plane(z), :] = (0.5 * NEAR * xz).astype(BF16)
        eout[6 * step + 5, plane(z), :] = (NEAR * zz).astype(BF16)

    def planes_loop(body):
        def step(z, carry):
            body(z)
            return carry

        lax.fori_loop(0, depth, step, 0, unroll=2)

    outs = []

    def put(src, dst):
        copy = pltpu.make_async_copy(src, dst, out_sem.at[len(outs)])
        copy.start()
        outs.append(copy)

    for f in (1, 3, 4):
        stress_load[f].wait()
    fill_rows(0, {})
    for f in (0, 2):
        stress_load[f].wait()
    send_columns(0, STRESS, s0)
    stress_load[5].wait()

    neighbours = 1 + sum(e.astype(jnp.int32) for e in (has_prev_y, has_next_y, has_prev_z, has_next_z))
    pl.semaphore_wait(barrier, neighbours)
    start_rows(0)
    columns_copy(0).start()
    start_planes(0)

    for copy in (buoy_load, vel_load, lam_load, mu_load):
        copy.wait()

    def scale(z):
        gain = per_plane(gain_ref, z)
        for ref in (buoy, lam, mu):
            ref[plane(z), :] = gain * ref[plane(z), :]

    planes_loop(scale)

    def old_motion(ref):
        if ref is vin:
            return lambda k, z: vin[k, plane(z), :]
        return lambda k, z: ref[k, plane(z + EDGE), :]

    for step in range(STEPS):
        last = step == STEPS - 1
        e = 2 * step
        src, old, new = (s0, vin, v1) if step == 0 else (s1, v1, v2)
        columns_copy(e).wait_recv()
        place_columns(e, STRESS)
        wait_planes(e)
        planes_loop(functools.partial(motion_plane, src, old_motion(old), new))
        wait_rows(e)
        values = {}
        for k, terms in enumerate(row_terms(e)):
            for y, term in terms.items():
                got = row_at(new, k, y)[...] + cell_row(buoy, y)[...] * term
                row_at(new, k, y)[...] = got
                values[k, y] = got
        fill_rows(e + 1, values)
        start_rows(e + 1)
        start_planes(e + 1)
        send_columns(e + 1, MOTION, new)
        columns_copy(e + 1).start()
        if last:
            for k in range(3):
                put(interior(new, k), vout_hbm.at[k])

        e = e + 1
        src, old = (v1, s0) if step == 0 else (v2, s1)

        def old_tensor(f, z, ref=old):
            return ref[f, plane(z + EDGE), :]

        def store(f, z, value):
            if last:
                sfin[f, plane(z), :] = value
            else:
                s1[f, plane(z + EDGE), :] = value

        def tensor_row(f, y):
            return cell_row(sfin.at[f], y) if last else row_at(s1, f, y)

        columns_copy(e).wait_recv()
        place_columns(e, MOTION)
        wait_planes(e)
        planes_loop(functools.partial(tensor_plane, src, old_tensor, store, step))
        for f in (0, 2, 5):
            put(eout.at[6 * step + f], eout_hbm.at[step, f])
        if last:
            put(sfin.at[2], sout_hbm.at[2])
        wait_rows(e)
        values = {}

        def raise_row(f, y, amount):
            got = tensor_row(f, y)[...] + amount
            tensor_row(f, y)[...] = got
            values[f, y] = got

        for k, terms in enumerate(row_terms(e)):
            for y, term in terms.items():
                stored = cell_row(strain.at[k], y)
                stored[...] = stored[...] + term
                mu_row = cell_row(mu, y)[...]
                if k == 1:
                    spread = cell_row(lam, y)[...] * term
                    raise_row(0, y, spread)
                    raise_row(5, y, spread)
                    raise_row(3, y, spread + (mu_row + mu_row) * term)
                else:
                    raise_row(1 if k == 0 else 4, y, mu_row * term)
        if last:
            for f in (1, 4, 3, 0, 5):
                put(sfin.at[f], sout_hbm.at[f])
        else:
            fill_rows(e + 1, values)
            start_rows(e + 1)
            start_planes(e + 1)
            send_columns(e + 1, STRESS, s1)
            columns_copy(e + 1).start()

        def convert(z):
            for k, f, factor in ((0, 1, 0.5 * NEAR), (1, 3, NEAR), (2, 4, 0.5 * NEAR)):
                eout[6 * step + f, plane(z), :] = (factor * strain[k, plane(z), :]).astype(BF16)

        planes_loop(convert)
        for f in (1, 3, 4):
            put(eout.at[6 * step + f], eout_hbm.at[step, f])

    for e in range(2 * STEPS):
        kind = kinds[e]
        columns_copy(e).wait_send()
        pl.when(has_next_y)(lambda: rows_copy(e, True, len(row_list(kind, True))).wait_send())
        pl.when(has_prev_y)(lambda: rows_copy(e, False, len(row_list(kind, False))).wait_send())
        for exists, upward in ((has_next_z, True), (has_prev_z, False)):
            @pl.when(exists)
            def _():
                for copy in planes_copies(e, kinds[e], refs[e], upward):
                    copy.wait_send()
    for copy in outs:
        copy.wait()


def on_device(velocity, stress, buoyancy, lame_lambda, shear_modulus, pml_flag, profile_index, damping_peak):
    _, depth, rows, lanes = velocity.shape
    exchanges = 2 * STEPS
    cells = depth * rows
    any_spec = pl.BlockSpec(memory_space=pl.ANY)
    smem_spec = pl.BlockSpec(memory_space=pltpu.SMEM)
    dma = pltpu.SemaphoreType.DMA

    def fields(count):
        return pltpu.VMEM((count, (depth + 2 * EDGE) * rows, lanes), F32)

    vout, sout, eout = pl.pallas_call(
        functools.partial(kernel, depth, rows, lanes),
        out_shape=(
            jax.ShapeDtypeStruct((3, cells, lanes), F32),
            jax.ShapeDtypeStruct((6, cells, lanes), F32),
            jax.ShapeDtypeStruct((STEPS, 6, cells, lanes), BF16),
        ),
        in_specs=[any_spec] * 5 + [smem_spec] * 3,
        out_specs=(any_spec,) * 3,
        scratch_shapes=[
            fields(6),
            fields(6),
            fields(3),
            fields(3),
            pltpu.VMEM((6, cells, lanes), F32),
            pltpu.VMEM((3, cells, lanes), F32),
            pltpu.VMEM((cells, lanes), F32),
            pltpu.VMEM((cells, lanes), F32),
            pltpu.VMEM((cells, lanes), F32),
            pltpu.VMEM((depth, 8, lanes), F32),
            pltpu.VMEM((depth, 8, lanes), F32),
            pltpu.VMEM((3, cells, lanes), F32),
            pltpu.VMEM((3, cells, lanes), F32),
            pltpu.VMEM((6 * STEPS, cells, lanes), BF16),
            pltpu.VMEM((exchanges, 5, depth, lanes), F32),
            pltpu.VMEM((exchanges, 5, depth, lanes), F32),
            pltpu.VMEM((exchanges, 5, depth, lanes), F32),
            pltpu.VMEM((exchanges, 5, depth, lanes), F32),
            pltpu.VMEM((exchanges, 8, cells), F32),
            pltpu.VMEM((exchanges, 8, cells), F32),
            dma((10,)),
            dma((32,)),
            dma((exchanges, 2)),
            dma((exchanges, 2)),
            dma((exchanges, 2, 3)),
            dma((exchanges, 2, 3)),
            dma((exchanges,)),
            dma((exchanges,)),
        ],
        compiler_params=pltpu.CompilerParams(collective_id=0, has_side_effects=True),
        name="two_steps",
    )(
        velocity.reshape(3, cells, lanes),
        stress.reshape(6, cells, lanes),
        buoyancy.reshape(cells, lanes),
        lame_lambda.reshape(cells, lanes),
        shear_modulus.reshape(cells, lanes),
        pml_flag,
        profile_index,
        damping_peak,
    )
    return (
        vout.reshape(velocity.shape),
        sout.reshape(stress.shape),
        eout.reshape(STEPS, *stress.shape),
    )


def solution(mesh):
    return jax.shard_map(
        on_device,
        mesh=mesh,
        in_specs=(
            P(None, "gy", "gx", "grp"),
            P(None, "gy", "gx", "grp"),
            P("gy", "gx", "grp"),
            P("gy", "gx", "grp"),
            P("gy", "gx", "grp"),
            P("gy", "gx", "grp"),
            P("gy", "gx", "grp"),
            P(),
        ),
        out_specs=(
            P(None, "gy", "gx", "grp"),
            P(None, "gy", "gx", "grp"),
            P(None, None, "gy", "gx", "grp"),
        ),
        check_vma=False,
    )
```

```python
import functools

import jax
import jax.numpy as jnp
from jax import lax
from jax.experimental import pallas as pl
from jax.experimental.pallas import tpu as pltpu
from jax.sharding import PartitionSpec as P

MESH = pl.DeviceIdType.MESH
F32 = jnp.float32
BF16 = jnp.bfloat16

STEPS = 2
NEAR = 9.0 / 8.0
RATIO = -1.0 / 27.0
TIME_STEP = 0.15
HALF = 0.5 * TIME_STEP

EDGE = 2

VMEM_LIMIT = 24 * 1024 * 1024

STRESS = {
    "x": ((0, True), (1, False), (2, False)),
    "y": ((1, False), (3, True), (4, False)),
    "z": ((2, False), (4, False), (5, True)),
}
MOTION = {
    "x": ((0, False), (1, True), (2, True)),
    "y": ((0, True), (1, False), (2, True)),
    "z": ((0, True), (1, True), (2, False)),
}


STRAIN = {"x": (0, 1, 2), "y": (1, 3, 4), "z": (2, 4, 5)}
NORMAL = (0, 3, 5)


def row_list(kind, upward):
    rows = [(slot, field, 0) for slot, (field, forward) in enumerate(kind["y"])]
    rows += [(slot, field, 1) for slot, (field, forward) in enumerate(kind["y"]) if forward != upward]
    return rows


def plane_list(kind, upward):
    runs, place = [], 0
    for field, forward in kind["z"]:
        count = 1 if forward == upward else 2
        runs.append((field, count, place))
        place += count
    return runs


def halo_terms(forward, before, after, length):
    if forward:
        return {
            0: -RATIO * before[0],
            length - 1: after[0] + RATIO * after[1],
            length - 2: RATIO * after[0],
        }
    return {
        0: -before[0] - RATIO * before[1],
        1: -RATIO * before[0],
        length - 1: RATIO * after[0],
    }


def kernel(
    depth, rows, lanes,
    vel_hbm, str_hbm, buoy_hbm, lam_hbm, mu_hbm, peak_hbm, flag_ref, prof_ref,
    v2, sfin, eout,
    s0, s1, v1, vin, buoy, lam, mu, keep_ref, gain_ref, strain, peak_ref,
    up_send, up_recv, dn_send, dn_recv, zup_recv, zdn_recv, grp_send, grp_recv,
    in_sem, ysend_sem, yrecv_sem, zsend_sem, zrecv_sem, gsend_sem, grecv_sem,
):
    gx, gy, grp = lax.axis_index("gx"), lax.axis_index("gy"), lax.axis_index("grp")
    n_gx, n_gy = lax.axis_size("gx"), lax.axis_size("gy")
    has_prev_y, has_next_y = gx > 0, gx < n_gx - 1
    has_prev_z, has_next_z = gy > 0, gy < n_gy - 1
    prev_y, next_y = {"gx": gx - 1}, {"gx": gx + 1}
    prev_z, next_z = {"gy": gy - 1}, {"gy": gy + 1}
    other = {"grp": 1 - grp}

    barrier = pltpu.get_barrier_semaphore()

    def greet(device):
        pl.semaphore_signal(barrier, inc=1, device_id=device, device_id_type=MESH)

    greet(other)
    for exists, device in (
        (has_prev_y, prev_y), (has_next_y, next_y), (has_prev_z, prev_z), (has_next_z, next_z),
    ):
        pl.when(exists)(functools.partial(greet, device))

    def planes(ref, field, first, count):
        return ref.at[field, pl.ds(first * rows, count * rows), :]

    def interior(ref, field):
        return planes(ref, field, EDGE, depth)

    def plane(p):
        return pl.ds(pl.multiple_of(p * rows, 8), rows)

    loads = []

    def load(src, dst):
        copy = pltpu.make_async_copy(src, dst, in_sem.at[len(loads)])
        copy.start()
        loads.append(copy)
        return copy

    stress_load = {f: load(str_hbm.at[f], interior(s0, f)) for f in (1, 3, 4, 0, 2, 5)}
    buoy_load = load(buoy_hbm, buoy)
    vel_load = load(vel_hbm, vin)
    lam_load = load(lam_hbm, lam)
    mu_load = load(mu_hbm, mu)
    peak_load = load(peak_hbm, peak_ref)

    for ref, fields in ((s0, (2, 4, 5)), (s1, (2, 4, 5)), (v1, (0, 1, 2)), (v2, (0, 1, 2))):
        for f in fields:
            for first in (0, EDGE + depth):
                ref[f, pl.ds(first * rows, EDGE * rows), :] = jnp.zeros((EDGE * rows, lanes), F32)

    def clear_recv(*refs):
        for ref in refs:
            ref[...] = jnp.zeros_like(ref)

    pl.when(jnp.logical_not(has_prev_y))(functools.partial(clear_recv, up_recv))
    pl.when(jnp.logical_not(has_next_y))(functools.partial(clear_recv, dn_recv))
    pl.when(jnp.logical_not(has_prev_z))(functools.partial(clear_recv, zup_recv))
    pl.when(jnp.logical_not(has_next_z))(functools.partial(clear_recv, zdn_recv))

    def set_damping():
        choice = prof_ref[0, 0, 0]
        peak = jnp.float32(0.0)
        for i in range(peak_ref.shape[0]):
            peak = peak + jnp.where(choice == i, peak_ref[i], 0.0)
        rate = flag_ref[0, 0, 0].astype(F32) * peak
        z = (lax.broadcasted_iota(jnp.int32, (depth, 8, lanes), 0) + gy * depth).astype(F32)
        q = (z + 0.5) / (depth * n_gy)
        damping = rate * (0.5 + 0.5 * q * q)
        divide = 1.0 + HALF * damping
        keep_ref[...] = (1.0 - HALF * damping) / divide
        gain_ref[...] = (NEAR * TIME_STEP) / divide

    slot = lax.broadcasted_iota(jnp.int32, (8, lanes), 0)
    lane = lax.broadcasted_iota(jnp.int32, (8, lanes), 1)
    near_lane = jnp.where(grp == 0, lanes - 1, 0)
    far_lane = jnp.where(grp == 0, lanes - 2, 1)

    def picker(k):
        hit = ((slot == 2 * k) & (lane == near_lane)) | ((slot == 2 * k + 1) & (lane == far_lane))
        return jnp.where(hit, 1.0, 0.0).astype(BF16)

    def placer(k, forward):
        near, far = slot == 2 * k, slot == 2 * k + 1
        if forward:
            one = (near & (lane == lanes - 1)) & (grp == 0)
            after = ((near & (lane == lanes - 2)) | (far & (lane == lanes - 1))) & (grp == 0)
            before = (near & (lane == 0)) & (grp == 1)
            whole = jnp.where(one, 1.0, 0.0)
        else:
            one = (near & (lane == 0)) & (grp == 1)
            after = (near & (lane == lanes - 1)) & (grp == 0)
            before = ((near & (lane == 1)) | (far & (lane == 0))) & (grp == 1)
            whole = jnp.where(one, -1.0, 0.0)
        part = jnp.where(after, RATIO, jnp.where(before, -RATIO, 0.0))
        high = part.astype(BF16)
        low = (part - high.astype(F32)).astype(BF16)
        return jnp.concatenate([whole.astype(BF16) + high, low], axis=0)

    def send_columns(e, kind, ref):
        total = None
        for k, (f, _) in enumerate(kind["x"]):
            cells = ref[f, pl.ds(EDGE * rows, depth * rows), :]
            term = lax.dot_general(
                picker(k), cells.astype(BF16), (((1,), (1,)), ((), ())), preferred_element_type=F32
            )
            total = term if total is None else total + term
        grp_send[e] = total

    def columns_copy(e):
        return pltpu.make_async_remote_copy(
            src_ref=grp_send.at[e], dst_ref=grp_recv.at[e], send_sem=gsend_sem.at[e], recv_sem=grecv_sem.at[e],
            device_id=other, device_id_type=MESH,
        )

    def column_terms(e):
        got = grp_recv[e].astype(BF16)
        pair = jnp.concatenate([got, got], axis=0)
        return [
            lax.dot_general(pair, placer(k, forward), (((0,), (0,)), ((), ())), preferred_element_type=F32)
            for k, (_, forward) in enumerate(kinds[e]["x"])
        ]

    def row_at(ref, field, y):
        return ref.at[field, pl.ds(EDGE * rows + y, depth, stride=rows), :]

    def cell_row(ref, y):
        return ref.at[pl.ds(y, depth, stride=rows), :]

    def rows_copy(e, upward, count):
        src, dst = (up_send, up_recv) if upward else (dn_send, dn_recv)
        way = 0 if upward else 1
        return pltpu.make_async_remote_copy(
            src_ref=src.at[e, pl.ds(0, count)], dst_ref=dst.at[e, pl.ds(0, count)],
            send_sem=ysend_sem.at[e, way], recv_sem=yrecv_sem.at[e, way],
            device_id=next_y if upward else prev_y, device_id_type=MESH,
        )

    def planes_copies(e, upward):
        way, dst = (0, zup_recv) if upward else (1, zdn_recv)
        copies = []
        for k, (f, count, place) in enumerate(plane_list(kinds[e], upward)):
            first = EDGE + depth - count if upward else EDGE
            copies.append(pltpu.make_async_remote_copy(
                src_ref=planes(refs[e], f, first, count),
                dst_ref=dst.at[e, pl.ds(place * rows, count * rows), :],
                send_sem=zsend_sem.at[e, way, k], recv_sem=zrecv_sem.at[e, way, k],
                device_id=next_z if upward else prev_z, device_id_type=MESH,
            ))
        return copies

    kinds = (STRESS, MOTION) * STEPS
    refs = (s0, v1, s1, v2)

    def start_rows(e):
        kind = kinds[e]
        pl.when(has_next_y)(lambda: rows_copy(e, True, len(row_list(kind, True))).start())
        pl.when(has_prev_y)(lambda: rows_copy(e, False, len(row_list(kind, False))).start())

    def start_planes(e):
        for exists, upward in ((has_next_z, True), (has_prev_z, False)):
            @pl.when(exists)
            def _():
                for copy in planes_copies(e, upward):
                    copy.start()

    def wait_planes(e):
        for exists, upward in ((has_prev_z, True), (has_next_z, False)):
            @pl.when(exists)
            def _():
                for copy in planes_copies(e, upward):
                    copy.wait_recv()

    def wait_rows(e):
        kind = kinds[e]
        pl.when(has_prev_y)(lambda: rows_copy(e, True, len(row_list(kind, True))).wait_recv())
        pl.when(has_next_y)(lambda: rows_copy(e, False, len(row_list(kind, False))).wait_recv())

    def row_terms(e):
        kind = kinds[e]
        before = {(k, far): up_recv[e, place] for place, (k, _, far) in enumerate(row_list(kind, True))}
        after = {(k, far): dn_recv[e, place] for place, (k, _, far) in enumerate(row_list(kind, False))}
        return [
            halo_terms(
                forward,
                [before[k, far] for far in range(2) if (k, far) in before],
                [after[k, far] for far in range(2) if (k, far) in after],
                rows,
            )
            for k, (_, forward) in enumerate(kind["y"])
        ]

    def plane_terms(e):
        kind = kinds[e]
        terms = []
        for k, (_, forward) in enumerate(kind["z"]):
            layers = []
            for upward, ref in ((True, zup_recv), (False, zdn_recv)):
                _, count, place = plane_list(kind, upward)[k]
                got = [ref[e, pl.ds((place + i) * rows, rows), :] for i in range(count)]
                layers.append(got[::-1] if upward else got)
            terms.append(halo_terms(forward, *layers, depth))
        return terms

    def fill_rows(e, values):
        kind, ref = kinds[e], refs[e]

        def value(field, y):
            got = values.get((field, y))
            return row_at(ref, field, y)[...] if got is None else got

        for place, (_, field, far) in enumerate(row_list(kind, True)):
            up_send[e, place] = value(field, rows - 1 - far)
        for place, (_, field, far) in enumerate(row_list(kind, False)):
            dn_send[e, place] = value(field, far)

    lane_id = lax.broadcasted_iota(jnp.int32, (rows, lanes), 1)
    row_id = lax.broadcasted_iota(jnp.int32, (rows, lanes), 0)

    def along_x(ref, field, p, forward):
        cells = ref[field, plane(p), :]
        one_back = jnp.where(lane_id >= 1, pltpu.roll(cells, 1, 1), 0.0)
        one_on = jnp.where(lane_id < lanes - 1, pltpu.roll(cells, lanes - 1, 1), 0.0)
        if forward:
            two_on = jnp.where(lane_id < lanes - 2, pltpu.roll(cells, lanes - 2, 1), 0.0)
            return one_on - cells, two_on - one_back
        two_back = jnp.where(lane_id >= 2, pltpu.roll(cells, 2, 1), 0.0)
        return cells - one_back, one_on - two_back

    def along_y(ref, field, p, forward):
        start = pl.multiple_of(p * rows, 8)

        def at(d):
            cells = ref[field, pl.ds(start + d, rows), :]
            if d == 0:
                return cells
            inside = row_id >= -d if d < 0 else row_id < rows - d
            return jnp.where(inside, cells, 0.0)

        if forward:
            return at(1) - at(0), at(2) - at(-1)
        return at(0) - at(-1), at(1) - at(-2)

    def along_z(ref, field, p, forward):
        at = lambda d: ref[field, plane(p + d), :]
        if forward:
            return at(1) - at(0), at(2) - at(-1)
        return at(0) - at(-1), at(1) - at(-2)

    def per_plane(ref, z):
        block = ref[z]
        return jnp.concatenate([block] * (rows // 8), axis=0)

    def inner(ref, z):
        return ref[plane(z), :]

    def joined(*parts):
        near = functools.reduce(lambda a, b: a + b, [n for n, _ in parts])
        far = functools.reduce(lambda a, b: a + b, [f for _, f in parts])
        return near + RATIO * far

    def motion_plane(src, old, new, z):
        p = z + EDGE
        keep, weight = per_plane(keep_ref, z), inner(buoy, z)
        cases = (
            ((along_x, 0, True), (along_y, 1, False), (along_z, 2, False)),
            ((along_x, 1, False), (along_y, 3, True), (along_z, 4, False)),
            ((along_x, 2, False), (along_y, 4, False), (along_z, 5, True)),
        )
        for k, case in enumerate(cases):
            force = joined(*[way(src, f, p, fwd) for way, f, fwd in case])
            new[k, plane(p), :] = keep * old(k, z) + weight * force

    def tensor_plane(src, old, store, z):
        p = z + EDGE
        keep, lam_z, mu_z = per_plane(keep_ref, z), inner(lam, z), inner(mu, z)
        xx = joined(along_x(src, 0, p, False))
        yy = joined(along_y(src, 1, p, False))
        zz = joined(along_z(src, 2, p, False))
        xy = joined(along_y(src, 0, p, True), along_x(src, 1, p, True))
        xz = joined(along_z(src, 0, p, True), along_x(src, 2, p, True))
        yz = joined(along_z(src, 1, p, True), along_y(src, 2, p, True))
        spread = lam_z * (xx + yy + zz)
        twice = mu_z + mu_z
        store(0, z, keep * old(0, z) + (spread + twice * xx))
        store(1, z, keep * old(1, z) + mu_z * xy)
        store(2, z, keep * old(2, z) + mu_z * xz)
        store(3, z, keep * old(3, z) + (spread + twice * yy))
        store(4, z, keep * old(4, z) + mu_z * yz)
        store(5, z, keep * old(5, z) + (spread + twice * zz))
        for f, value in enumerate((xx, xy, xz, yy, yz, zz)):
            strain[f, plane(z), :] = value

    def planes_loop(body):
        def step(z, carry):
            body(z)
            return carry

        lax.fori_loop(0, depth, step, 0, unroll=2)

    for f in (1, 3, 4):
        stress_load[f].wait()
    fill_rows(0, {})
    for f in (0, 2):
        stress_load[f].wait()
    send_columns(0, STRESS, s0)
    stress_load[5].wait()

    neighbours = 1 + sum(e.astype(jnp.int32) for e in (has_prev_y, has_next_y, has_prev_z, has_next_z))
    pl.semaphore_wait(barrier, neighbours)
    start_rows(0)
    columns_copy(0).start()
    start_planes(0)

    for copy in (peak_load, buoy_load, vel_load, lam_load, mu_load):
        copy.wait()
    set_damping()

    def scale(z):
        gain = per_plane(gain_ref, z)
        for ref in (buoy, lam, mu):
            ref[plane(z), :] = gain * ref[plane(z), :]

    planes_loop(scale)

    def old_motion(ref):
        if ref is vin:
            return lambda k, z: vin[k, plane(z), :]
        return lambda k, z: ref[k, plane(z + EDGE), :]

    for step in range(STEPS):
        last = step == STEPS - 1
        e = 2 * step
        src, old, new = (s0, vin, v1) if step == 0 else (s1, v1, v2)
        planes_loop(functools.partial(motion_plane, src, old_motion(old), new))
        wait_planes(e)
        for k, terms in enumerate(plane_terms(e)):
            for z, term in terms.items():
                cells = new.at[k, pl.ds((z + EDGE) * rows, rows), :]
                cells[...] = cells[...] + buoy[pl.ds(z * rows, rows), :] * term
        columns_copy(e).wait_recv()
        for k, term in enumerate(column_terms(e)):
            cells = interior(new, k)
            cells[...] = cells[...] + buoy[...] * term
        wait_rows(e)
        values = {}
        for k, terms in enumerate(row_terms(e)):
            for y, term in terms.items():
                got = row_at(new, k, y)[...] + cell_row(buoy, y)[...] * term
                row_at(new, k, y)[...] = got
                values[k, y] = got
        fill_rows(e + 1, values)
        start_rows(e + 1)
        start_planes(e + 1)
        send_columns(e + 1, MOTION, new)
        columns_copy(e + 1).start()

        e = e + 1
        src, old = (v1, s0) if step == 0 else (v2, s1)

        def old_tensor(f, z, ref=old):
            return ref[f, plane(z + EDGE), :]

        def store(f, z, value):
            if last:
                sfin[f, plane(z), :] = value
            else:
                s1[f, plane(z + EDGE), :] = value

        def correct(component, term, stress_at, cell_at, strain_at):
            changed = {}
            place = strain_at(component)
            place[...] = place[...] + term
            shear = cell_at(mu)[...] * term
            if component in NORMAL:
                spread = cell_at(lam)[...] * term
                for f in NORMAL:
                    changed[f] = spread + (shear + shear) if f == component else spread
            else:
                changed[component] = shear
            for f, amount in changed.items():
                changed[f] = stress_at(f)[...] + amount
                stress_at(f)[...] = changed[f]
            return changed

        def convert(components):
            def body(z):
                for f in components:
                    factor = NEAR if f in NORMAL else 0.5 * NEAR
                    eout[6 * step + f, plane(z), :] = (factor * strain[f, plane(z), :]).astype(BF16)

            planes_loop(body)

        planes_loop(functools.partial(tensor_plane, src, old_tensor, store))
        wait_planes(e)
        for k, terms in enumerate(plane_terms(e)):
            for z, term in terms.items():
                cell = pl.ds(z * rows, rows)
                correct(
                    STRAIN["z"][k], term,
                    lambda f: sfin.at[f, cell, :] if last else s1.at[f, pl.ds((z + EDGE) * rows, rows), :],
                    lambda ref: ref.at[cell, :],
                    lambda f: strain.at[f, cell, :],
                )
        columns_copy(e).wait_recv()
        for k, term in enumerate(column_terms(e)):
            correct(
                STRAIN["x"][k], term,
                lambda f: sfin.at[f] if last else interior(s1, f),
                lambda ref: ref,
                lambda f: strain.at[f],
            )
        if last:
            convert((0, 2, 5))
        wait_rows(e)
        values = {}
        for k, terms in enumerate(row_terms(e)):
            for y, term in terms.items():
                changed = correct(
                    STRAIN["y"][k], term,
                    lambda f: cell_row(sfin.at[f], y) if last else row_at(s1, f, y),
                    lambda ref: cell_row(ref, y),
                    lambda f: cell_row(strain.at[f], y),
                )
                for f, got in changed.items():
                    values[f, y] = got
        if last:
            convert((1, 3, 4))
        else:
            fill_rows(e + 1, values)
            start_rows(e + 1)
            start_planes(e + 1)
            send_columns(e + 1, STRESS, s1)
            columns_copy(e + 1).start()
            convert(range(6))

    for e in range(2 * STEPS):
        kind = kinds[e]
        columns_copy(e).wait_send()
        pl.when(has_next_y)(lambda: rows_copy(e, True, len(row_list(kind, True))).wait_send())
        pl.when(has_prev_y)(lambda: rows_copy(e, False, len(row_list(kind, False))).wait_send())
        for exists, upward in ((has_next_z, True), (has_prev_z, False)):
            @pl.when(exists)
            def _():
                for copy in planes_copies(e, upward):
                    copy.wait_send()


def write_out(v2, sfin, eout, vout_hbm, sout_hbm, eout_hbm, sem):
    cells = vout_hbm.shape[1]
    edge = (v2.shape[1] - cells) // 2
    copies = []

    def put(src, dst):
        copies.append(pltpu.make_async_copy(src, dst, sem.at[len(copies)]))
        copies[-1].start()

    for f in range(6):
        put(sfin.at[f], sout_hbm.at[f])
    for f in range(3):
        put(v2.at[f, pl.ds(edge, cells), :], vout_hbm.at[f])
    for f in range(6 * STEPS):
        put(eout.at[f], eout_hbm.at[f])
    for copy in copies:
        copy.wait()


def on_device(velocity, stress, buoyancy, lame_lambda, shear_modulus, pml_flag, profile_index, damping_peak):
    _, depth, rows, lanes = velocity.shape
    exchanges = 2 * STEPS
    cells = depth * rows
    any_spec = pl.BlockSpec(memory_space=pl.ANY)
    vmem_spec = pl.BlockSpec(memory_space=pltpu.VMEM)
    dma = pltpu.SemaphoreType.DMA
    halo_cells = (depth + 2 * EDGE) * rows

    def fields(count):
        return pltpu.VMEM((count, halo_cells, lanes), F32)

    final = pl.pallas_call(
        functools.partial(kernel, depth, rows, lanes),
        out_shape=(
            jax.ShapeDtypeStruct((3, halo_cells, lanes), F32),
            jax.ShapeDtypeStruct((6, cells, lanes), F32),
            jax.ShapeDtypeStruct((6 * STEPS, cells, lanes), BF16),
        ),
        in_specs=[any_spec] * 6 + [pl.BlockSpec(memory_space=pltpu.SMEM)] * 2,
        out_specs=(vmem_spec,) * 3,
        scratch_shapes=[
            fields(6),
            fields(6),
            fields(3),
            pltpu.VMEM((3, cells, lanes), F32),
            pltpu.VMEM((cells, lanes), F32),
            pltpu.VMEM((cells, lanes), F32),
            pltpu.VMEM((cells, lanes), F32),
            pltpu.VMEM((depth, 8, lanes), F32),
            pltpu.VMEM((depth, 8, lanes), F32),
            pltpu.VMEM((6, cells, lanes), F32),
            pltpu.SMEM(damping_peak.shape, F32),
            pltpu.VMEM((exchanges, 5, depth, lanes), F32),
            pltpu.VMEM((exchanges, 5, depth, lanes), F32),
            pltpu.VMEM((exchanges, 5, depth, lanes), F32),
            pltpu.VMEM((exchanges, 5, depth, lanes), F32),
            pltpu.VMEM((exchanges, 5 * rows, lanes), F32),
            pltpu.VMEM((exchanges, 5 * rows, lanes), F32),
            pltpu.VMEM((exchanges, 8, cells), F32),
            pltpu.VMEM((exchanges, 8, cells), F32),
            dma((11,)),
            dma((exchanges, 2)),
            dma((exchanges, 2)),
            dma((exchanges, 2, 3)),
            dma((exchanges, 2, 3)),
            dma((exchanges,)),
            dma((exchanges,)),
        ],
        compiler_params=pltpu.CompilerParams(
            collective_id=0, has_side_effects=True, vmem_limit_bytes=VMEM_LIMIT
        ),
        name="two_steps",
    )(
        *[
            pltpu.with_memory_space_constraint(x, pltpu.HBM)
            for x in (
                velocity.reshape(3, cells, lanes),
                stress.reshape(6, cells, lanes),
                buoyancy.reshape(cells, lanes),
                lame_lambda.reshape(cells, lanes),
                shear_modulus.reshape(cells, lanes),
                damping_peak,
            )
        ],
        pml_flag,
        profile_index,
    )
    vout, sout, eout = pl.pallas_call(
        write_out,
        out_shape=(
            jax.ShapeDtypeStruct((3, cells, lanes), F32),
            jax.ShapeDtypeStruct((6, cells, lanes), F32),
            jax.ShapeDtypeStruct((6 * STEPS, cells, lanes), BF16),
        ),
        in_specs=[any_spec] * 3,
        out_specs=(any_spec,) * 3,
        scratch_shapes=[dma((9 + 6 * STEPS,))],
        compiler_params=pltpu.CompilerParams(vmem_limit_bytes=VMEM_LIMIT),
        name="write_out",
    )(*final)
    return (
        vout.reshape(velocity.shape),
        sout.reshape(stress.shape),
        eout.reshape(STEPS, *stress.shape),
    )


def solution(mesh):
    return jax.shard_map(
        on_device,
        mesh=mesh,
        in_specs=(
            P(None, "gy", "gx", "grp"),
            P(None, "gy", "gx", "grp"),
            P("gy", "gx", "grp"),
            P("gy", "gx", "grp"),
            P("gy", "gx", "grp"),
            P("gy", "gx", "grp"),
            P("gy", "gx", "grp"),
            P(),
        ),
        out_specs=(
            P(None, "gy", "gx", "grp"),
            P(None, "gy", "gx", "grp"),
            P(None, None, "gy", "gx", "grp"),
        ),
        check_vma=False,
    )
```

```python
import functools

import jax
import jax.numpy as jnp
from jax import lax
from jax.experimental import pallas as pl
from jax.experimental.pallas import tpu as pltpu
from jax.sharding import PartitionSpec as P

MESH = pl.DeviceIdType.MESH
F32 = jnp.float32
BF16 = jnp.bfloat16

STEPS = 2
NEAR = 9.0 / 8.0
RATIO = -1.0 / 27.0
TIME_STEP = 0.15
HALF = 0.5 * TIME_STEP

EDGE = 2

VMEM_LIMIT = 24 * 1024 * 1024

STRESS = {
    "x": ((0, True), (1, False), (2, False)),
    "y": ((1, False), (3, True), (4, False)),
    "z": ((2, False), (4, False), (5, True)),
}
MOTION = {
    "x": ((0, False), (1, True), (2, True)),
    "y": ((0, True), (1, False), (2, True)),
    "z": ((0, True), (1, True), (2, False)),
}


STRAIN = {"x": (0, 1, 2), "y": (1, 3, 4), "z": (2, 4, 5)}
NORMAL = (0, 3, 5)


def whole_list(fields, upward):
    return [k for k, (_, forward) in enumerate(fields) if forward != upward]


def part_depth(forward, upward):
    return 1 if forward != upward else 0


def halo_terms(forward, before, after, length):
    if forward:
        return {
            0: -RATIO * before[0],
            length - 1: after[0] + RATIO * after[1],
            length - 2: RATIO * after[0],
        }
    return {
        0: -before[0] - RATIO * before[1],
        1: -RATIO * before[0],
        length - 1: RATIO * after[0],
    }


def kernel(
    depth, rows, lanes,
    vel_hbm, str_hbm, buoy_hbm, lam_hbm, mu_hbm, peak_hbm, flag_ref, prof_ref,
    v2, sfin, eout,
    s0, s1, v1, vin, buoy, lam, mu, keep_ref, gain_ref, strain, peak_ref,
    ywhole_send, ywhole_recv, ypart_send, ypart_recv, zwhole_send, zwhole_recv, zpart_send, zpart_recv,
    grp_send, grp_recv,
    in_sem, ysend_sem, yrecv_sem, zsend_sem, zrecv_sem, gsend_sem, grecv_sem,
):
    gx, gy, grp = lax.axis_index("gx"), lax.axis_index("gy"), lax.axis_index("grp")
    n_gx, n_gy = lax.axis_size("gx"), lax.axis_size("gy")
    has_prev_y, has_next_y = gx > 0, gx < n_gx - 1
    has_prev_z, has_next_z = gy > 0, gy < n_gy - 1
    prev_y, next_y = {"gx": gx - 1}, {"gx": gx + 1}
    prev_z, next_z = {"gy": gy - 1}, {"gy": gy + 1}
    other = {"grp": 1 - grp}

    barrier = pltpu.get_barrier_semaphore()

    def greet(device):
        pl.semaphore_signal(barrier, inc=1, device_id=device, device_id_type=MESH)

    greet(other)
    for exists, device in (
        (has_prev_y, prev_y), (has_next_y, next_y), (has_prev_z, prev_z), (has_next_z, next_z),
    ):
        pl.when(exists)(functools.partial(greet, device))

    def planes(ref, field, first, count):
        return ref.at[field, pl.ds(first * rows, count * rows), :]

    def interior(ref, field):
        return planes(ref, field, EDGE, depth)

    def plane(p):
        return pl.ds(pl.multiple_of(p * rows, 8), rows)

    loads = []

    def load(src, dst):
        copy = pltpu.make_async_copy(src, dst, in_sem.at[len(loads)])
        copy.start()
        loads.append(copy)
        return copy

    stress_load = {f: load(str_hbm.at[f], interior(s0, f)) for f in (1, 3, 4, 2, 5, 0)}
    buoy_load = load(buoy_hbm, buoy)
    vel_load = load(vel_hbm, vin)
    lam_load = load(lam_hbm, lam)
    mu_load = load(mu_hbm, mu)
    peak_load = load(peak_hbm, peak_ref)

    for ref, fields in ((s0, (2, 4, 5)), (s1, (2, 4, 5)), (v1, (0, 1, 2)), (v2, (0, 1, 2))):
        for f in fields:
            for first in (0, EDGE + depth):
                ref[f, pl.ds(first * rows, EDGE * rows), :] = jnp.zeros((EDGE * rows, lanes), F32)

    def clear_recv(way, *refs):
        for ref in refs:
            for e in range(2 * STEPS):
                ref[e, way] = jnp.zeros(ref.shape[2:], ref.dtype)

    for exists, way, refs_of in (
        (has_prev_y, 0, (ywhole_recv, ypart_recv)),
        (has_next_y, 1, (ywhole_recv, ypart_recv)),
        (has_prev_z, 0, (zwhole_recv, zpart_recv)),
        (has_next_z, 1, (zwhole_recv, zpart_recv)),
    ):
        pl.when(jnp.logical_not(exists))(functools.partial(clear_recv, way, *refs_of))

    def set_damping():
        choice = prof_ref[0, 0, 0]
        peak = jnp.float32(0.0)
        for i in range(peak_ref.shape[0]):
            peak = peak + jnp.where(choice == i, peak_ref[i], 0.0)
        rate = flag_ref[0, 0, 0].astype(F32) * peak
        z = (lax.broadcasted_iota(jnp.int32, (depth, 8, lanes), 0) + gy * depth).astype(F32)
        q = (z + 0.5) / (depth * n_gy)
        damping = rate * (0.5 + 0.5 * q * q)
        divide = 1.0 + HALF * damping
        keep_ref[...] = (1.0 - HALF * damping) / divide
        gain_ref[...] = (NEAR * TIME_STEP) / divide

    slot = lax.broadcasted_iota(jnp.int32, (8, lanes), 0)
    lane = lax.broadcasted_iota(jnp.int32, (8, lanes), 1)
    near_lane = jnp.where(grp == 0, lanes - 1, 0)
    far_lane = jnp.where(grp == 0, lanes - 2, 1)

    def picker(k):
        hit = ((slot == 2 * k) & (lane == near_lane)) | ((slot == 2 * k + 1) & (lane == far_lane))
        return jnp.where(hit, 1.0, 0.0).astype(BF16)

    def placer(k, forward):
        near, far = slot == 2 * k, slot == 2 * k + 1
        if forward:
            one = (near & (lane == lanes - 1)) & (grp == 0)
            after = ((near & (lane == lanes - 2)) | (far & (lane == lanes - 1))) & (grp == 0)
            before = (near & (lane == 0)) & (grp == 1)
            whole = jnp.where(one, 1.0, 0.0)
        else:
            one = (near & (lane == 0)) & (grp == 1)
            after = (near & (lane == lanes - 1)) & (grp == 0)
            before = ((near & (lane == 1)) | (far & (lane == 0))) & (grp == 1)
            whole = jnp.where(one, -1.0, 0.0)
        part = jnp.where(after, RATIO, jnp.where(before, -RATIO, 0.0))
        high = part.astype(BF16)
        low = (part - high.astype(F32)).astype(BF16)
        return jnp.concatenate([whole.astype(BF16) + high, low], axis=0)

    def send_columns(e, kind, ref):
        total = None
        for k, (f, _) in enumerate(kind["x"]):
            cells = ref[f, pl.ds(EDGE * rows, depth * rows), :]
            term = lax.dot_general(
                picker(k), cells.astype(BF16), (((1,), (1,)), ((), ())), preferred_element_type=F32
            )
            total = term if total is None else total + term
        grp_send[e] = total.astype(BF16)

    def columns_copy(e):
        return pltpu.make_async_remote_copy(
            src_ref=grp_send.at[e], dst_ref=grp_recv.at[e], send_sem=gsend_sem.at[e], recv_sem=grecv_sem.at[e],
            device_id=other, device_id_type=MESH,
        )

    def column_terms(e):
        got = grp_recv[e]
        pair = jnp.concatenate([got, got], axis=0)
        return [
            lax.dot_general(pair, placer(k, forward), (((0,), (0,)), ((), ())), preferred_element_type=F32)
            for k, (_, forward) in enumerate(kinds[e]["x"])
        ]

    def row_at(ref, field, y):
        return ref.at[field, pl.ds(EDGE * rows + y, depth, stride=rows), :]

    def cell_row(ref, y):
        return ref.at[pl.ds(y, depth, stride=rows), :]

    kinds = (STRESS, MOTION) * STEPS
    refs = (s0, v1, s1, v2)
    axes = {
        "y": (
            ywhole_send, ywhole_recv, ypart_send, ypart_recv, ysend_sem, yrecv_sem,
            has_prev_y, has_next_y, prev_y, next_y,
        ),
        "z": (
            zwhole_send, zwhole_recv, zpart_send, zpart_recv, zsend_sem, zrecv_sem,
            has_prev_z, has_next_z, prev_z, next_z,
        ),
    }

    def face_copies(e, axis, upward):
        whole, whole_to, part, part_to, send_sem, recv_sem, _, _, before, after = axes[axis]
        way = 0 if upward else 1
        count = len(whole_list(kinds[e][axis], upward))
        return [
            pltpu.make_async_remote_copy(
                src_ref=src, dst_ref=dst, send_sem=send_sem.at[e, way, i], recv_sem=recv_sem.at[e, way, i],
                device_id=after if upward else before, device_id_type=MESH,
            )
            for i, (src, dst) in enumerate((
                (whole.at[e, way, pl.ds(0, count)], whole_to.at[e, way, pl.ds(0, count)]),
                (part.at[e, way], part_to.at[e, way]),
            ))
        ]

    def each_copy(e, axis, outgoing, act):
        has_before, has_after = axes[axis][6:8]
        for exists, upward in ((has_after, outgoing), (has_before, not outgoing)):
            @pl.when(exists)
            def _():
                for copy in face_copies(e, axis, upward):
                    act(copy)

    def start_faces(e, axis):
        each_copy(e, axis, True, lambda copy: copy.start())

    def wait_faces(e, axis):
        each_copy(e, axis, False, lambda copy: copy.wait_recv())

    def fill_faces(e, axis, value):
        whole, _, part, _ = axes[axis][:4]
        fields = kinds[e][axis]
        for way, upward in ((0, True), (1, False)):
            last_index = (rows if axis == "y" else depth) - 1

            def layer(k, far):
                return value(fields[k][0], last_index - far if upward else far)

            for place, k in enumerate(whole_list(fields, upward)):
                whole[e, way, place] = layer(k, 0)
            for k, (_, forward) in enumerate(fields):
                part[e, way, k] = layer(k, part_depth(forward, upward)).astype(BF16)

    def fill_rows(e, values):
        fill_faces(e, "y", lambda f, y: row_at(refs[e], f, y)[...] if (f, y) not in values else values[f, y])

    def fill_planes(e):
        fill_faces(e, "z", lambda f, z: refs[e][f, pl.ds((z + EDGE) * rows, rows), :])

    def face_terms(e, axis):
        _, whole, _, part = axes[axis][:4]
        fields = kinds[e][axis]
        terms = []
        for k, (_, forward) in enumerate(fields):
            layers = []
            for way, upward in ((0, True), (1, False)):
                got = [part[e, way, k].astype(F32)]
                if forward != upward:
                    got.insert(0, whole[e, way, whole_list(fields, upward).index(k)])
                layers.append(got)
            terms.append(halo_terms(forward, *layers, rows if axis == "y" else depth))
        return terms

    lane_id = lax.broadcasted_iota(jnp.int32, (rows, lanes), 1)
    row_id = lax.broadcasted_iota(jnp.int32, (rows, lanes), 0)

    def along_x(ref, field, p, forward):
        cells = ref[field, plane(p), :]
        one_back = jnp.where(lane_id >= 1, pltpu.roll(cells, 1, 1), 0.0)
        one_on = jnp.where(lane_id < lanes - 1, pltpu.roll(cells, lanes - 1, 1), 0.0)
        if forward:
            two_on = jnp.where(lane_id < lanes - 2, pltpu.roll(cells, lanes - 2, 1), 0.0)
            return one_on - cells, two_on - one_back
        two_back = jnp.where(lane_id >= 2, pltpu.roll(cells, 2, 1), 0.0)
        return cells - one_back, one_on - two_back

    def along_y(ref, field, p, forward):
        start = pl.multiple_of(p * rows, 8)

        def at(d):
            cells = ref[field, pl.ds(start + d, rows), :]
            if d == 0:
                return cells
            inside = row_id >= -d if d < 0 else row_id < rows - d
            return jnp.where(inside, cells, 0.0)

        if forward:
            return at(1) - at(0), at(2) - at(-1)
        return at(0) - at(-1), at(1) - at(-2)

    def along_z(ref, field, p, forward):
        at = lambda d: ref[field, plane(p + d), :]
        if forward:
            return at(1) - at(0), at(2) - at(-1)
        return at(0) - at(-1), at(1) - at(-2)

    def per_plane(ref, z):
        block = ref[z]
        return jnp.concatenate([block] * (rows // 8), axis=0)

    def inner(ref, z):
        return ref[plane(z), :]

    def joined(*parts):
        near = functools.reduce(lambda a, b: a + b, [n for n, _ in parts])
        far = functools.reduce(lambda a, b: a + b, [f for _, f in parts])
        return near + RATIO * far

    def motion_plane(src, old, new, z):
        p = z + EDGE
        keep, weight = per_plane(keep_ref, z), inner(buoy, z)
        cases = (
            ((along_x, 0, True), (along_y, 1, False), (along_z, 2, False)),
            ((along_x, 1, False), (along_y, 3, True), (along_z, 4, False)),
            ((along_x, 2, False), (along_y, 4, False), (along_z, 5, True)),
        )
        for k, case in enumerate(cases):
            force = joined(*[way(src, f, p, fwd) for way, f, fwd in case])
            new[k, plane(p), :] = keep * old(k, z) + weight * force

    def tensor_plane(src, old, store, z):
        p = z + EDGE
        keep, lam_z, mu_z = per_plane(keep_ref, z), inner(lam, z), inner(mu, z)
        xx = joined(along_x(src, 0, p, False))
        yy = joined(along_y(src, 1, p, False))
        zz = joined(along_z(src, 2, p, False))
        xy = joined(along_y(src, 0, p, True), along_x(src, 1, p, True))
        xz = joined(along_z(src, 0, p, True), along_x(src, 2, p, True))
        yz = joined(along_z(src, 1, p, True), along_y(src, 2, p, True))
        spread = lam_z * (xx + yy + zz)
        twice = mu_z + mu_z
        store(0, z, keep * old(0, z) + (spread + twice * xx))
        store(1, z, keep * old(1, z) + mu_z * xy)
        store(2, z, keep * old(2, z) + mu_z * xz)
        store(3, z, keep * old(3, z) + (spread + twice * yy))
        store(4, z, keep * old(4, z) + mu_z * yz)
        store(5, z, keep * old(5, z) + (spread + twice * zz))
        for f, value in enumerate((xx, xy, xz, yy, yz, zz)):
            strain[f, plane(z), :] = value

    def planes_loop(body):
        def step(z, carry):
            body(z)
            return carry

        lax.fori_loop(0, depth, step, 0, unroll=2)

    for f in (1, 3, 4):
        stress_load[f].wait()
    fill_rows(0, {})
    for f in (2, 5):
        stress_load[f].wait()
    fill_planes(0)
    stress_load[0].wait()

    neighbours = 1 + sum(e.astype(jnp.int32) for e in (has_prev_y, has_next_y, has_prev_z, has_next_z))
    pl.semaphore_wait(barrier, neighbours)
    start_faces(0, "y")
    start_faces(0, "z")
    send_columns(0, STRESS, s0)
    columns_copy(0).start()

    for copy in (peak_load, buoy_load, vel_load, lam_load, mu_load):
        copy.wait()
    set_damping()

    def scale(z):
        gain = per_plane(gain_ref, z)
        for ref in (buoy, lam, mu):
            ref[plane(z), :] = gain * ref[plane(z), :]

    planes_loop(scale)

    def old_motion(ref):
        if ref is vin:
            return lambda k, z: vin[k, plane(z), :]
        return lambda k, z: ref[k, plane(z + EDGE), :]

    for step in range(STEPS):
        last = step == STEPS - 1
        e = 2 * step
        src, old, new = (s0, vin, v1) if step == 0 else (s1, v1, v2)
        planes_loop(functools.partial(motion_plane, src, old_motion(old), new))
        columns_copy(e).wait_recv()
        for k, term in enumerate(column_terms(e)):
            cells = interior(new, k)
            cells[...] = cells[...] + buoy[...] * term
        wait_faces(e, "z")
        for k, terms in enumerate(face_terms(e, "z")):
            for z, term in terms.items():
                cells = new.at[k, pl.ds((z + EDGE) * rows, rows), :]
                cells[...] = cells[...] + buoy[pl.ds(z * rows, rows), :] * term
        wait_faces(e, "y")
        values = {}
        for k, terms in enumerate(face_terms(e, "y")):
            for y, term in terms.items():
                got = row_at(new, k, y)[...] + cell_row(buoy, y)[...] * term
                row_at(new, k, y)[...] = got
                values[k, y] = got
        fill_rows(e + 1, values)
        start_faces(e + 1, "y")
        fill_planes(e + 1)
        start_faces(e + 1, "z")
        send_columns(e + 1, MOTION, new)
        columns_copy(e + 1).start()

        e = e + 1
        src, old = (v1, s0) if step == 0 else (v2, s1)

        def old_tensor(f, z, ref=old):
            return ref[f, plane(z + EDGE), :]

        def store(f, z, value):
            if last:
                sfin[f, plane(z), :] = value
            else:
                s1[f, plane(z + EDGE), :] = value

        def correct(component, term, stress_at, cell_at, strain_at):
            changed = {}
            place = strain_at(component)
            place[...] = place[...] + term
            shear = cell_at(mu)[...] * term
            if component in NORMAL:
                spread = cell_at(lam)[...] * term
                for f in NORMAL:
                    changed[f] = spread + (shear + shear) if f == component else spread
            else:
                changed[component] = shear
            for f, amount in changed.items():
                changed[f] = stress_at(f)[...] + amount
                stress_at(f)[...] = changed[f]
            return changed

        def convert(components):
            def body(z):
                for f in components:
                    factor = NEAR if f in NORMAL else 0.5 * NEAR
                    eout[6 * step + f, plane(z), :] = (factor * strain[f, plane(z), :]).astype(BF16)

            planes_loop(body)

        planes_loop(functools.partial(tensor_plane, src, old_tensor, store))
        columns_copy(e).wait_recv()
        for k, term in enumerate(column_terms(e)):
            correct(
                STRAIN["x"][k], term,
                lambda f: sfin.at[f] if last else interior(s1, f),
                lambda ref: ref,
                lambda f: strain.at[f],
            )
        wait_faces(e, "z")
        for k, terms in enumerate(face_terms(e, "z")):
            for z, term in terms.items():
                cell = pl.ds(z * rows, rows)
                correct(
                    STRAIN["z"][k], term,
                    lambda f: sfin.at[f, cell, :] if last else s1.at[f, pl.ds((z + EDGE) * rows, rows), :],
                    lambda ref: ref.at[cell, :],
                    lambda f: strain.at[f, cell, :],
                )
        if last:
            convert((0, 2, 5))
        wait_faces(e, "y")

        def stress_row(f, y):
            return cell_row(sfin.at[f], y) if last else row_at(s1, f, y)

        def change(f, y, amount):
            got = stress_row(f, y)[...] + amount
            stress_row(f, y)[...] = got
            return got

        shear_xy, normal_y, shear_yz = face_terms(e, "y")
        values, spread = {}, {}
        for f, terms in ((1, shear_xy), (4, shear_yz)):
            for y, term in terms.items():
                values[f, y] = change(f, y, cell_row(mu, y)[...] * term)
        for y, term in normal_y.items():
            mu_row = cell_row(mu, y)[...]
            spread[y] = cell_row(lam, y)[...] * term
            values[3, y] = change(3, y, spread[y] + (mu_row + mu_row) * term)
        if not last:
            fill_rows(e + 1, values)
            start_faces(e + 1, "y")
        for y, amount in spread.items():
            change(5, y, amount)
        if not last:
            fill_planes(e + 1)
            start_faces(e + 1, "z")
        for y, amount in spread.items():
            change(0, y, amount)
        if not last:
            send_columns(e + 1, STRESS, s1)
            columns_copy(e + 1).start()
        for f, terms in ((1, shear_xy), (3, normal_y), (4, shear_yz)):
            for y, term in terms.items():
                place = cell_row(strain.at[f], y)
                place[...] = place[...] + term
        convert((1, 3, 4) if last else range(6))

    for e in range(2 * STEPS):
        columns_copy(e).wait_send()
        for axis in axes:
            each_copy(e, axis, True, lambda copy: copy.wait_send())


def write_out(v2, sfin, eout, vout_hbm, sout_hbm, eout_hbm, sem):
    cells = vout_hbm.shape[1]
    edge = (v2.shape[1] - cells) // 2
    copies = []

    def put(src, dst):
        copies.append(pltpu.make_async_copy(src, dst, sem.at[len(copies)]))
        copies[-1].start()

    for f in range(6):
        put(sfin.at[f], sout_hbm.at[f])
    for f in range(3):
        put(v2.at[f, pl.ds(edge, cells), :], vout_hbm.at[f])
    for f in range(6 * STEPS):
        put(eout.at[f], eout_hbm.at[f])
    for copy in copies:
        copy.wait()


def on_device(velocity, stress, buoyancy, lame_lambda, shear_modulus, pml_flag, profile_index, damping_peak):
    _, depth, rows, lanes = velocity.shape
    exchanges = 2 * STEPS
    cells = depth * rows
    any_spec = pl.BlockSpec(memory_space=pl.ANY)
    vmem_spec = pl.BlockSpec(memory_space=pltpu.VMEM)
    dma = pltpu.SemaphoreType.DMA
    halo_cells = (depth + 2 * EDGE) * rows

    def fields(count):
        return pltpu.VMEM((count, halo_cells, lanes), F32)

    final = pl.pallas_call(
        functools.partial(kernel, depth, rows, lanes),
        out_shape=(
            jax.ShapeDtypeStruct((3, halo_cells, lanes), F32),
            jax.ShapeDtypeStruct((6, cells, lanes), F32),
            jax.ShapeDtypeStruct((6 * STEPS, cells, lanes), BF16),
        ),
        in_specs=[any_spec] * 6 + [pl.BlockSpec(memory_space=pltpu.SMEM)] * 2,
        out_specs=(vmem_spec,) * 3,
        scratch_shapes=[
            fields(6),
            fields(6),
            fields(3),
            pltpu.VMEM((3, cells, lanes), F32),
            pltpu.VMEM((cells, lanes), F32),
            pltpu.VMEM((cells, lanes), F32),
            pltpu.VMEM((cells, lanes), F32),
            pltpu.VMEM((depth, 8, lanes), F32),
            pltpu.VMEM((depth, 8, lanes), F32),
            pltpu.VMEM((6, cells, lanes), F32),
            pltpu.SMEM(damping_peak.shape, F32),
            *[pltpu.VMEM((exchanges, 2, 2, depth, lanes), F32)] * 2,
            *[pltpu.VMEM((exchanges, 2, 3, depth, lanes), BF16)] * 2,
            *[pltpu.VMEM((exchanges, 2, 2, rows, lanes), F32)] * 2,
            *[pltpu.VMEM((exchanges, 2, 3, rows, lanes), BF16)] * 2,
            *[pltpu.VMEM((exchanges, 8, cells), BF16)] * 2,
            dma((11,)),
            *[dma((exchanges, 2, 2))] * 4,
            *[dma((exchanges,))] * 2,
        ],
        compiler_params=pltpu.CompilerParams(
            collective_id=0, has_side_effects=True, vmem_limit_bytes=VMEM_LIMIT
        ),
        name="two_steps",
    )(
        *[
            pltpu.with_memory_space_constraint(x, pltpu.HBM)
            for x in (
                velocity.reshape(3, cells, lanes),
                stress.reshape(6, cells, lanes),
                buoyancy.reshape(cells, lanes),
                lame_lambda.reshape(cells, lanes),
                shear_modulus.reshape(cells, lanes),
                damping_peak,
            )
        ],
        pml_flag,
        profile_index,
    )
    vout, sout, eout = pl.pallas_call(
        write_out,
        out_shape=(
            jax.ShapeDtypeStruct((3, cells, lanes), F32),
            jax.ShapeDtypeStruct((6, cells, lanes), F32),
            jax.ShapeDtypeStruct((6 * STEPS, cells, lanes), BF16),
        ),
        in_specs=[any_spec] * 3,
        out_specs=(any_spec,) * 3,
        scratch_shapes=[dma((9 + 6 * STEPS,))],
        compiler_params=pltpu.CompilerParams(vmem_limit_bytes=VMEM_LIMIT),
        name="write_out",
    )(*final)
    return (
        vout.reshape(velocity.shape),
        sout.reshape(stress.shape),
        eout.reshape(STEPS, *stress.shape),
    )


def solution(mesh):
    return jax.shard_map(
        on_device,
        mesh=mesh,
        in_specs=(
            P(None, "gy", "gx", "grp"),
            P(None, "gy", "gx", "grp"),
            P("gy", "gx", "grp"),
            P("gy", "gx", "grp"),
            P("gy", "gx", "grp"),
            P("gy", "gx", "grp"),
            P("gy", "gx", "grp"),
            P(),
        ),
        out_specs=(
            P(None, "gy", "gx", "grp"),
            P(None, "gy", "gx", "grp"),
            P(None, None, "gy", "gx", "grp"),
        ),
        check_vma=False,
    )
```

```python
import functools

import jax
import jax.numpy as jnp
from jax import lax
from jax.experimental import pallas as pl
from jax.experimental.pallas import tpu as pltpu
from jax.sharding import PartitionSpec as P

MESH = pl.DeviceIdType.MESH
F32 = jnp.float32
BF16 = jnp.bfloat16

STEPS = 2
NEAR = 9.0 / 8.0
RATIO = -1.0 / 27.0
TIME_STEP = 0.15
HALF = 0.5 * TIME_STEP

EDGE = 2

VMEM_LIMIT = 24 * 1024 * 1024

STRESS = {
    "x": ((0, True), (1, False), (2, False)),
    "y": ((1, False), (3, True), (4, False)),
    "z": ((2, False), (4, False), (5, True)),
}
MOTION = {
    "x": ((0, False), (1, True), (2, True)),
    "y": ((0, True), (1, False), (2, True)),
    "z": ((0, True), (1, True), (2, False)),
}


STRAIN = {"x": (0, 1, 2), "y": (1, 3, 4), "z": (2, 4, 5)}
NORMAL = (0, 3, 5)


def whole_list(fields, upward):
    return [k for k, (_, forward) in enumerate(fields) if forward != upward]


def part_depth(forward, upward):
    return 1 if forward != upward else 0


def halo_terms(forward, before, after, length):
    if forward:
        return {
            0: -RATIO * before[0],
            length - 1: after[0] + RATIO * after[1],
            length - 2: RATIO * after[0],
        }
    return {
        0: -before[0] - RATIO * before[1],
        1: -RATIO * before[0],
        length - 1: RATIO * after[0],
    }


def kernel(
    depth, rows, lanes,
    vel_hbm, str_hbm, buoy_hbm, lam_hbm, mu_hbm, peak_hbm, flag_ref, prof_ref,
    v2, sfin, eout,
    s0, s1, v1, vin, buoy, lam, mu, keep_ref, gain_ref, strain, peak_ref,
    ywhole_send, ywhole_recv, ypart_send, ypart_recv, zwhole_send, zwhole_recv, zpart_send, zpart_recv,
    coef_send, coef_recv, grp_send, grp_recv,
    in_sem, ysend_sem, yrecv_sem, zsend_sem, zrecv_sem, csend_sem, crecv_sem, gsend_sem, grecv_sem,
):
    gx, gy, grp = lax.axis_index("gx"), lax.axis_index("gy"), lax.axis_index("grp")
    n_gx, n_gy = lax.axis_size("gx"), lax.axis_size("gy")
    has_prev_y, has_next_y = gx > 0, gx < n_gx - 1
    has_prev_z, has_next_z = gy > 0, gy < n_gy - 1
    prev_y, next_y = {"gx": gx - 1}, {"gx": gx + 1}
    prev_z, next_z = {"gy": gy - 1}, {"gy": gy + 1}
    other = {"grp": 1 - grp}

    barrier = pltpu.get_barrier_semaphore()

    def greet(device):
        pl.semaphore_signal(barrier, inc=1, device_id=device, device_id_type=MESH)

    greet(other)
    for exists, device in (
        (has_prev_y, prev_y), (has_next_y, next_y), (has_prev_z, prev_z), (has_next_z, next_z),
    ):
        pl.when(exists)(functools.partial(greet, device))

    def planes(ref, field, first, count):
        return ref.at[field, pl.ds(first * rows, count * rows), :]

    def interior(ref, field):
        return planes(ref, field, EDGE, depth)

    def plane(p):
        return pl.ds(pl.multiple_of(p * rows, 8), rows)

    loads = []

    def load(src, dst):
        copy = pltpu.make_async_copy(src, dst, in_sem.at[len(loads)])
        copy.start()
        loads.append(copy)
        return copy

    stress_load = {f: load(str_hbm.at[f], interior(s0, f)) for f in (1, 3, 4, 2, 5, 0)}
    buoy_load = load(buoy_hbm, buoy)
    vel_load = load(vel_hbm, vin)
    lam_load = load(lam_hbm, lam)
    mu_load = load(mu_hbm, mu)
    peak_load = load(peak_hbm, peak_ref)

    for ref, fields in ((s0, (2, 4, 5)), (s1, (2, 4, 5)), (v1, (0, 1, 2)), (v2, (0, 1, 2))):
        for f in fields:
            for first in (0, EDGE + depth):
                ref[f, pl.ds(first * rows, EDGE * rows), :] = jnp.zeros((EDGE * rows, lanes), F32)

    def clear_recv(way, *refs):
        for ref in refs:
            for e in range(2 * STEPS):
                ref[e, way] = jnp.zeros(ref.shape[2:], ref.dtype)

    for exists, way, refs_of in (
        (has_prev_y, 0, (ywhole_recv, ypart_recv)),
        (has_next_y, 1, (ywhole_recv, ypart_recv)),
        (has_prev_z, 0, (zwhole_recv, zpart_recv)),
        (has_next_z, 1, (zwhole_recv, zpart_recv)),
    ):
        pl.when(jnp.logical_not(exists))(functools.partial(clear_recv, way, *refs_of))

    def clear_coef(way):
        coef_recv[way] = jnp.zeros(coef_recv.shape[1:], F32)

    pl.when(jnp.logical_not(has_prev_y))(functools.partial(clear_coef, 0))
    pl.when(jnp.logical_not(has_next_y))(functools.partial(clear_coef, 1))

    def set_damping():
        choice = prof_ref[0, 0, 0]
        peak = jnp.float32(0.0)
        for i in range(peak_ref.shape[0]):
            peak = peak + jnp.where(choice == i, peak_ref[i], 0.0)
        rate = flag_ref[0, 0, 0].astype(F32) * peak
        z = (lax.broadcasted_iota(jnp.int32, (depth, 8, lanes), 0) + gy * depth).astype(F32)
        q = (z + 0.5) / (depth * n_gy)
        damping = rate * (0.5 + 0.5 * q * q)
        divide = 1.0 + HALF * damping
        keep_ref[...] = (1.0 - HALF * damping) / divide
        gain_ref[...] = (NEAR * TIME_STEP) / divide

    slot = lax.broadcasted_iota(jnp.int32, (8, lanes), 0)
    lane = lax.broadcasted_iota(jnp.int32, (8, lanes), 1)
    near_lane = jnp.where(grp == 0, lanes - 1, 0)
    far_lane = jnp.where(grp == 0, lanes - 2, 1)

    def picker(k):
        hit = ((slot == 2 * k) & (lane == near_lane)) | ((slot == 2 * k + 1) & (lane == far_lane))
        return jnp.where(hit, 1.0, 0.0).astype(BF16)

    def placer(k, forward):
        near, far = slot == 2 * k, slot == 2 * k + 1
        if forward:
            one = (near & (lane == lanes - 1)) & (grp == 0)
            after = ((near & (lane == lanes - 2)) | (far & (lane == lanes - 1))) & (grp == 0)
            before = (near & (lane == 0)) & (grp == 1)
            whole = jnp.where(one, 1.0, 0.0)
        else:
            one = (near & (lane == 0)) & (grp == 1)
            after = (near & (lane == lanes - 1)) & (grp == 0)
            before = ((near & (lane == 1)) | (far & (lane == 0))) & (grp == 1)
            whole = jnp.where(one, -1.0, 0.0)
        part = jnp.where(after, RATIO, jnp.where(before, -RATIO, 0.0))
        high = part.astype(BF16)
        low = (part - high.astype(F32)).astype(BF16)
        return jnp.concatenate([whole.astype(BF16) + high, low], axis=0)

    def send_columns(e, kind, ref):
        total = None
        for k, (f, _) in enumerate(kind["x"]):
            cells = ref[f, pl.ds(EDGE * rows, depth * rows), :]
            term = lax.dot_general(
                picker(k), cells.astype(BF16), (((1,), (1,)), ((), ())), preferred_element_type=F32
            )
            total = term if total is None else total + term
        grp_send[e] = total.astype(BF16)

    def columns_copy(e):
        return pltpu.make_async_remote_copy(
            src_ref=grp_send.at[e], dst_ref=grp_recv.at[e], send_sem=gsend_sem.at[e], recv_sem=grecv_sem.at[e],
            device_id=other, device_id_type=MESH,
        )

    def column_terms(e):
        got = grp_recv[e]
        pair = jnp.concatenate([got, got], axis=0)
        return [
            lax.dot_general(pair, placer(k, forward), (((0,), (0,)), ((), ())), preferred_element_type=F32)
            for k, (_, forward) in enumerate(kinds[e]["x"])
        ]

    def row_at(ref, field, y):
        return ref.at[field, pl.ds(EDGE * rows + y, depth, stride=rows), :]

    def cell_row(ref, y):
        return ref.at[pl.ds(y, depth, stride=rows), :]

    kinds = (STRESS, MOTION) * STEPS
    refs = (s0, v1, s1, v2)
    axes = {
        "y": (
            ywhole_send, ywhole_recv, ypart_send, ypart_recv, ysend_sem, yrecv_sem,
            has_prev_y, has_next_y, prev_y, next_y,
        ),
        "z": (
            zwhole_send, zwhole_recv, zpart_send, zpart_recv, zsend_sem, zrecv_sem,
            has_prev_z, has_next_z, prev_z, next_z,
        ),
    }

    def face_copies(e, axis, upward):
        whole, whole_to, part, part_to, send_sem, recv_sem, _, _, before, after = axes[axis]
        way = 0 if upward else 1
        count = len(whole_list(kinds[e][axis], upward))
        return [
            pltpu.make_async_remote_copy(
                src_ref=src, dst_ref=dst, send_sem=send_sem.at[e, way, i], recv_sem=recv_sem.at[e, way, i],
                device_id=after if upward else before, device_id_type=MESH,
            )
            for i, (src, dst) in enumerate((
                (whole.at[e, way, pl.ds(0, count)], whole_to.at[e, way, pl.ds(0, count)]),
                (part.at[e, way], part_to.at[e, way]),
            ))
        ]

    def each_copy(e, axis, outgoing, act):
        has_before, has_after = axes[axis][6:8]
        for exists, upward in ((has_after, outgoing), (has_before, not outgoing)):
            @pl.when(exists)
            def _():
                for copy in face_copies(e, axis, upward):
                    act(copy)

    def start_faces(e, axis):
        each_copy(e, axis, True, lambda copy: copy.start())

    def wait_faces(e, axis):
        each_copy(e, axis, False, lambda copy: copy.wait_recv())

    def fill_faces(e, axis, value):
        whole, _, part, _ = axes[axis][:4]
        fields = kinds[e][axis]
        for way, upward in ((0, True), (1, False)):
            last_index = (rows if axis == "y" else depth) - 1

            def layer(k, far):
                return value(fields[k][0], last_index - far if upward else far)

            for place, k in enumerate(whole_list(fields, upward)):
                whole[e, way, place] = layer(k, 0)
            for k, (_, forward) in enumerate(fields):
                part[e, way, k] = layer(k, part_depth(forward, upward)).astype(BF16)

    def fill_rows(e):
        fill_faces(e, "y", lambda f, y: row_at(refs[e], f, y)[...])

    def fill_planes(e):
        fill_faces(e, "z", lambda f, z: refs[e][f, pl.ds((z + EDGE) * rows, rows), :])

    def material_row(k, stress, y):
        if not stress:
            return cell_row(buoy, y)[...]
        if k == 1:
            mu_row = cell_row(mu, y)[...]
            return cell_row(lam, y)[...] + (mu_row + mu_row)
        return cell_row(mu, y)[...]

    def fill_material():
        for way, (near, far) in ((0, (rows - 1, rows - 2)), (1, (0, 1))):
            coef_send[way, 0] = material_row(0, False, near)
            coef_send[way, 1] = material_row(0, False, far)
            coef_send[way, 2] = material_row(0, True, near)
            coef_send[way, 3] = material_row(1, True, near)
            coef_send[way, 4] = material_row(way, True, far)

    def material_copy(way):
        return pltpu.make_async_remote_copy(
            src_ref=coef_send.at[way], dst_ref=coef_recv.at[way],
            send_sem=csend_sem.at[way], recv_sem=crecv_sem.at[way],
            device_id=prev_y if way else next_y, device_id_type=MESH,
        )

    def completions(e):
        if e == 0:
            return {}
        missing = {}
        for way, upward in ((0, True), (1, False)):
            near, far = (0, 1) if upward else (rows - 1, rows - 2)
            sign = 1.0 if upward else -1.0

            def coef(k, layer):
                if kinds[e] is MOTION:
                    return coef_recv[way, layer]
                return coef_recv[way, 4 if layer else (3 if k == 1 else 2)]

            for k, (_, forward) in enumerate(kinds[e]["y"]):
                driver = kinds[e - 1]["y"][k][0]
                near_row = row_at(refs[e - 1], driver, near)[...]
                part = (sign * RATIO) * near_row
                if forward != upward:
                    far_row = row_at(refs[e - 1], driver, far)[...]
                    missing[way, k, 0] = coef(k, 0) * (sign * near_row + (sign * RATIO) * far_row)
                    missing[way, k, 1] = coef(k, 1) * part
                else:
                    missing[way, k, 0] = coef(k, 0) * part
        return missing

    def face_terms(e, axis, missing=None):
        _, whole, _, part = axes[axis][:4]
        fields = kinds[e][axis]
        terms = []
        for k, (_, forward) in enumerate(fields):
            layers = []
            for way, upward in ((0, True), (1, False)):
                got = [part[e, way, k].astype(F32)]
                if forward != upward:
                    got.insert(0, whole[e, way, whole_list(fields, upward).index(k)])
                if missing:
                    got = [layer + missing[way, k, i] for i, layer in enumerate(got)]
                layers.append(got)
            terms.append(halo_terms(forward, *layers, rows if axis == "y" else depth))
        return terms

    lane_id = lax.broadcasted_iota(jnp.int32, (rows, lanes), 1)
    row_id = lax.broadcasted_iota(jnp.int32, (rows, lanes), 0)

    def along_x(ref, field, p, forward):
        cells = ref[field, plane(p), :]
        one_back = jnp.where(lane_id >= 1, pltpu.roll(cells, 1, 1), 0.0)
        one_on = jnp.where(lane_id < lanes - 1, pltpu.roll(cells, lanes - 1, 1), 0.0)
        if forward:
            two_on = jnp.where(lane_id < lanes - 2, pltpu.roll(cells, lanes - 2, 1), 0.0)
            return one_on - cells, two_on - one_back
        two_back = jnp.where(lane_id >= 2, pltpu.roll(cells, 2, 1), 0.0)
        return cells - one_back, one_on - two_back

    def along_y(ref, field, p, forward):
        start = pl.multiple_of(p * rows, 8)

        def at(d):
            cells = ref[field, pl.ds(start + d, rows), :]
            if d == 0:
                return cells
            inside = row_id >= -d if d < 0 else row_id < rows - d
            return jnp.where(inside, cells, 0.0)

        if forward:
            return at(1) - at(0), at(2) - at(-1)
        return at(0) - at(-1), at(1) - at(-2)

    def along_z(ref, field, p, forward):
        at = lambda d: ref[field, plane(p + d), :]
        if forward:
            return at(1) - at(0), at(2) - at(-1)
        return at(0) - at(-1), at(1) - at(-2)

    def per_plane(ref, z):
        block = ref[z]
        return jnp.concatenate([block] * (rows // 8), axis=0)

    def inner(ref, z):
        return ref[plane(z), :]

    def joined(*parts):
        near = functools.reduce(lambda a, b: a + b, [n for n, _ in parts])
        far = functools.reduce(lambda a, b: a + b, [f for _, f in parts])
        return near + RATIO * far

    def motion_plane(src, old, new, z):
        p = z + EDGE
        keep, weight = per_plane(keep_ref, z), inner(buoy, z)
        cases = (
            ((along_x, 0, True), (along_y, 1, False), (along_z, 2, False)),
            ((along_x, 1, False), (along_y, 3, True), (along_z, 4, False)),
            ((along_x, 2, False), (along_y, 4, False), (along_z, 5, True)),
        )
        for k, case in enumerate(cases):
            force = joined(*[way(src, f, p, fwd) for way, f, fwd in case])
            new[k, plane(p), :] = keep * old(k, z) + weight * force

    def tensor_plane(src, old, store, z):
        p = z + EDGE
        keep, lam_z, mu_z = per_plane(keep_ref, z), inner(lam, z), inner(mu, z)
        xx = joined(along_x(src, 0, p, False))
        yy = joined(along_y(src, 1, p, False))
        zz = joined(along_z(src, 2, p, False))
        xy = joined(along_y(src, 0, p, True), along_x(src, 1, p, True))
        xz = joined(along_z(src, 0, p, True), along_x(src, 2, p, True))
        yz = joined(along_z(src, 1, p, True), along_y(src, 2, p, True))
        spread = lam_z * (xx + yy + zz)
        twice = mu_z + mu_z
        store(0, z, keep * old(0, z) + (spread + twice * xx))
        store(1, z, keep * old(1, z) + mu_z * xy)
        store(2, z, keep * old(2, z) + mu_z * xz)
        store(3, z, keep * old(3, z) + (spread + twice * yy))
        store(4, z, keep * old(4, z) + mu_z * yz)
        store(5, z, keep * old(5, z) + (spread + twice * zz))
        for f, value in enumerate((xx, xy, xz, yy, yz, zz)):
            strain[f, plane(z), :] = value

    def planes_loop(body):
        def step(z, carry):
            body(z)
            return carry

        lax.fori_loop(0, depth, step, 0, unroll=2)

    for f in (1, 3, 4):
        stress_load[f].wait()
    fill_rows(0)
    for f in (2, 5):
        stress_load[f].wait()
    fill_planes(0)
    stress_load[0].wait()

    neighbours = 1 + sum(e.astype(jnp.int32) for e in (has_prev_y, has_next_y, has_prev_z, has_next_z))
    pl.semaphore_wait(barrier, neighbours)
    start_faces(0, "y")
    start_faces(0, "z")
    send_columns(0, STRESS, s0)
    columns_copy(0).start()

    for copy in (peak_load, buoy_load, vel_load, lam_load, mu_load):
        copy.wait()
    set_damping()

    def scale(z):
        gain = per_plane(gain_ref, z)
        for ref in (buoy, lam, mu):
            ref[plane(z), :] = gain * ref[plane(z), :]

    planes_loop(scale)
    fill_material()
    pl.when(has_next_y)(lambda: material_copy(0).start())
    pl.when(has_prev_y)(lambda: material_copy(1).start())

    def old_motion(ref):
        if ref is vin:
            return lambda k, z: vin[k, plane(z), :]
        return lambda k, z: ref[k, plane(z + EDGE), :]

    for step in range(STEPS):
        last = step == STEPS - 1
        e = 2 * step
        src, old, new = (s0, vin, v1) if step == 0 else (s1, v1, v2)
        planes_loop(functools.partial(motion_plane, src, old_motion(old), new))
        columns_copy(e).wait_recv()
        for k, term in enumerate(column_terms(e)):
            cells = interior(new, k)
            cells[...] = cells[...] + buoy[...] * term
        wait_faces(e, "z")
        for k, terms in enumerate(face_terms(e, "z")):
            for z, term in terms.items():
                cells = new.at[k, pl.ds((z + EDGE) * rows, rows), :]
                cells[...] = cells[...] + buoy[pl.ds(z * rows, rows), :] * term
        fill_rows(e + 1)
        start_faces(e + 1, "y")
        missing = completions(e)
        wait_faces(e, "y")
        for k, terms in enumerate(face_terms(e, "y", missing)):
            for y, term in terms.items():
                row_at(new, k, y)[...] = row_at(new, k, y)[...] + cell_row(buoy, y)[...] * term
        fill_planes(e + 1)
        start_faces(e + 1, "z")
        send_columns(e + 1, MOTION, new)
        columns_copy(e + 1).start()

        e = e + 1
        src, old = (v1, s0) if step == 0 else (v2, s1)

        def old_tensor(f, z, ref=old):
            return ref[f, plane(z + EDGE), :]

        def store(f, z, value):
            if last:
                sfin[f, plane(z), :] = value
            else:
                s1[f, plane(z + EDGE), :] = value

        def correct(component, term, stress_at, cell_at, strain_at):
            changed = {}
            place = strain_at(component)
            place[...] = place[...] + term
            shear = cell_at(mu)[...] * term
            if component in NORMAL:
                spread = cell_at(lam)[...] * term
                for f in NORMAL:
                    changed[f] = spread + (shear + shear) if f == component else spread
            else:
                changed[component] = shear
            for f, amount in changed.items():
                changed[f] = stress_at(f)[...] + amount
                stress_at(f)[...] = changed[f]
            return changed

        def convert(components):
            def body(z):
                for f in components:
                    factor = NEAR if f in NORMAL else 0.5 * NEAR
                    eout[6 * step + f, plane(z), :] = (factor * strain[f, plane(z), :]).astype(BF16)

            planes_loop(body)

        planes_loop(functools.partial(tensor_plane, src, old_tensor, store))
        columns_copy(e).wait_recv()
        for k, term in enumerate(column_terms(e)):
            correct(
                STRAIN["x"][k], term,
                lambda f: sfin.at[f] if last else interior(s1, f),
                lambda ref: ref,
                lambda f: strain.at[f],
            )
        wait_faces(e, "z")
        for k, terms in enumerate(face_terms(e, "z")):
            for z, term in terms.items():
                cell = pl.ds(z * rows, rows)
                correct(
                    STRAIN["z"][k], term,
                    lambda f: sfin.at[f, cell, :] if last else s1.at[f, pl.ds((z + EDGE) * rows, rows), :],
                    lambda ref: ref.at[cell, :],
                    lambda f: strain.at[f, cell, :],
                )
        if last:
            convert((0, 2, 5))
        else:
            fill_rows(e + 1)
            start_faces(e + 1, "y")
        if e == 1:
            pl.when(has_prev_y)(lambda: material_copy(0).wait_recv())
            pl.when(has_next_y)(lambda: material_copy(1).wait_recv())
        missing = completions(e)
        wait_faces(e, "y")

        def stress_row(f, y):
            return cell_row(sfin.at[f], y) if last else row_at(s1, f, y)

        def change(f, y, amount):
            got = stress_row(f, y)[...] + amount
            stress_row(f, y)[...] = got
            return got

        shear_xy, normal_y, shear_yz = face_terms(e, "y", missing)
        spread = {y: cell_row(lam, y)[...] * term for y, term in normal_y.items()}
        for y, term in shear_yz.items():
            change(4, y, cell_row(mu, y)[...] * term)
        for y, amount in spread.items():
            change(5, y, amount)
        if not last:
            fill_planes(e + 1)
            start_faces(e + 1, "z")
        for y, amount in spread.items():
            change(0, y, amount)
        for y, term in shear_xy.items():
            change(1, y, cell_row(mu, y)[...] * term)
        if not last:
            send_columns(e + 1, STRESS, s1)
            columns_copy(e + 1).start()
        for y, term in normal_y.items():
            mu_row = cell_row(mu, y)[...]
            change(3, y, spread[y] + (mu_row + mu_row) * term)
        for f, terms in ((1, shear_xy), (3, normal_y), (4, shear_yz)):
            for y, term in terms.items():
                place = cell_row(strain.at[f], y)
                place[...] = place[...] + term
        convert((1, 3, 4) if last else range(6))

    for e in range(2 * STEPS):
        columns_copy(e).wait_send()
        for axis in axes:
            each_copy(e, axis, True, lambda copy: copy.wait_send())
    pl.when(has_next_y)(lambda: material_copy(0).wait_send())
    pl.when(has_prev_y)(lambda: material_copy(1).wait_send())


def write_out(v2, sfin, eout, vout_hbm, sout_hbm, eout_hbm, sem):
    cells = vout_hbm.shape[1]
    edge = (v2.shape[1] - cells) // 2
    copies = []

    def put(src, dst):
        copies.append(pltpu.make_async_copy(src, dst, sem.at[len(copies)]))
        copies[-1].start()

    for f in range(6):
        put(sfin.at[f], sout_hbm.at[f])
    for f in range(3):
        put(v2.at[f, pl.ds(edge, cells), :], vout_hbm.at[f])
    for f in range(6 * STEPS):
        put(eout.at[f], eout_hbm.at[f])
    for copy in copies:
        copy.wait()


def on_device(velocity, stress, buoyancy, lame_lambda, shear_modulus, pml_flag, profile_index, damping_peak):
    _, depth, rows, lanes = velocity.shape
    exchanges = 2 * STEPS
    cells = depth * rows
    any_spec = pl.BlockSpec(memory_space=pl.ANY)
    vmem_spec = pl.BlockSpec(memory_space=pltpu.VMEM)
    dma = pltpu.SemaphoreType.DMA
    halo_cells = (depth + 2 * EDGE) * rows

    def fields(count):
        return pltpu.VMEM((count, halo_cells, lanes), F32)

    final = pl.pallas_call(
        functools.partial(kernel, depth, rows, lanes),
        out_shape=(
            jax.ShapeDtypeStruct((3, halo_cells, lanes), F32),
            jax.ShapeDtypeStruct((6, cells, lanes), F32),
            jax.ShapeDtypeStruct((6 * STEPS, cells, lanes), BF16),
        ),
        in_specs=[any_spec] * 6 + [pl.BlockSpec(memory_space=pltpu.SMEM)] * 2,
        out_specs=(vmem_spec,) * 3,
        scratch_shapes=[
            fields(6),
            fields(6),
            fields(3),
            pltpu.VMEM((3, cells, lanes), F32),
            pltpu.VMEM((cells, lanes), F32),
            pltpu.VMEM((cells, lanes), F32),
            pltpu.VMEM((cells, lanes), F32),
            pltpu.VMEM((depth, 8, lanes), F32),
            pltpu.VMEM((depth, 8, lanes), F32),
            pltpu.VMEM((6, cells, lanes), F32),
            pltpu.SMEM(damping_peak.shape, F32),
            *[pltpu.VMEM((exchanges, 2, 2, depth, lanes), F32)] * 2,
            *[pltpu.VMEM((exchanges, 2, 3, depth, lanes), BF16)] * 2,
            *[pltpu.VMEM((exchanges, 2, 2, rows, lanes), F32)] * 2,
            *[pltpu.VMEM((exchanges, 2, 3, rows, lanes), BF16)] * 2,
            *[pltpu.VMEM((2, 5, depth, lanes), F32)] * 2,
            *[pltpu.VMEM((exchanges, 8, cells), BF16)] * 2,
            dma((11,)),
            *[dma((exchanges, 2, 2))] * 4,
            *[dma((2,))] * 2,
            *[dma((exchanges,))] * 2,
        ],
        compiler_params=pltpu.CompilerParams(
            collective_id=0, has_side_effects=True, vmem_limit_bytes=VMEM_LIMIT
        ),
        name="two_steps",
    )(
        *[
            pltpu.with_memory_space_constraint(x, pltpu.HBM)
            for x in (
                velocity.reshape(3, cells, lanes),
                stress.reshape(6, cells, lanes),
                buoyancy.reshape(cells, lanes),
                lame_lambda.reshape(cells, lanes),
                shear_modulus.reshape(cells, lanes),
                damping_peak,
            )
        ],
        pml_flag,
        profile_index,
    )
    vout, sout, eout = pl.pallas_call(
        write_out,
        out_shape=(
            jax.ShapeDtypeStruct((3, cells, lanes), F32),
            jax.ShapeDtypeStruct((6, cells, lanes), F32),
            jax.ShapeDtypeStruct((6 * STEPS, cells, lanes), BF16),
        ),
        in_specs=[any_spec] * 3,
        out_specs=(any_spec,) * 3,
        scratch_shapes=[dma((9 + 6 * STEPS,))],
        compiler_params=pltpu.CompilerParams(vmem_limit_bytes=VMEM_LIMIT),
        name="write_out",
    )(*final)
    return (
        vout.reshape(velocity.shape),
        sout.reshape(stress.shape),
        eout.reshape(STEPS, *stress.shape),
    )


def solution(mesh):
    return jax.shard_map(
        on_device,
        mesh=mesh,
        in_specs=(
            P(None, "gy", "gx", "grp"),
            P(None, "gy", "gx", "grp"),
            P("gy", "gx", "grp"),
            P("gy", "gx", "grp"),
            P("gy", "gx", "grp"),
            P("gy", "gx", "grp"),
            P("gy", "gx", "grp"),
            P(),
        ),
        out_specs=(
            P(None, "gy", "gx", "grp"),
            P(None, "gy", "gx", "grp"),
            P(None, None, "gy", "gx", "grp"),
        ),
        check_vma=False,
    )
```

```python
import functools

import jax
import jax.numpy as jnp
from jax import lax
from jax.experimental import pallas as pl
from jax.experimental.pallas import tpu as pltpu
from jax.sharding import PartitionSpec as P

MESH = pl.DeviceIdType.MESH
F32 = jnp.float32
BF16 = jnp.bfloat16

STEPS = 2
NEAR = 9.0 / 8.0
RATIO = -1.0 / 27.0
TIME_STEP = 0.15
HALF = 0.5 * TIME_STEP

EDGE = 2

VMEM_LIMIT = 24 * 1024 * 1024

STRESS = {
    "x": ((0, True), (1, False), (2, False)),
    "y": ((1, False), (3, True), (4, False)),
    "z": ((2, False), (4, False), (5, True)),
}
MOTION = {
    "x": ((0, False), (1, True), (2, True)),
    "y": ((0, True), (1, False), (2, True)),
    "z": ((0, True), (1, True), (2, False)),
}


STRAIN = {"x": (0, 1, 2), "y": (1, 3, 4), "z": (2, 4, 5)}
NORMAL = (0, 3, 5)


def whole_list(fields, upward):
    return [k for k, (_, forward) in enumerate(fields) if forward != upward]


def part_depth(forward, upward):
    return 1 if forward != upward else 0


def halo_terms(forward, before, after, length):
    if forward:
        return {
            0: -RATIO * before[0],
            length - 1: after[0] + RATIO * after[1],
            length - 2: RATIO * after[0],
        }
    return {
        0: -before[0] - RATIO * before[1],
        1: -RATIO * before[0],
        length - 1: RATIO * after[0],
    }


def kernel(
    depth, rows, lanes,
    vel_hbm, str_hbm, buoy_hbm, lam_hbm, mu_hbm, peak_hbm, flag_ref, prof_ref,
    v2, sfin, eout,
    s0, s1, v1, vin, buoy, lam, mu, keep_ref, gain_ref, strain, peak_ref,
    ywhole_send, ywhole_recv, ypart_send, ypart_recv, zwhole_send, zwhole_recv, zpart_send, zpart_recv,
    coef_send, coef_recv, grp_send, grp_recv,
    in_sem, ysend_sem, yrecv_sem, zsend_sem, zrecv_sem, csend_sem, crecv_sem, gsend_sem, grecv_sem,
):
    gx, gy, grp = lax.axis_index("gx"), lax.axis_index("gy"), lax.axis_index("grp")
    n_gx, n_gy = lax.axis_size("gx"), lax.axis_size("gy")
    has_prev_y, has_next_y = gx > 0, gx < n_gx - 1
    has_prev_z, has_next_z = gy > 0, gy < n_gy - 1
    prev_y, next_y = {"gx": gx - 1}, {"gx": gx + 1}
    prev_z, next_z = {"gy": gy - 1}, {"gy": gy + 1}
    other = {"grp": 1 - grp}

    barrier = pltpu.get_barrier_semaphore()

    def greet(device):
        pl.semaphore_signal(barrier, inc=1, device_id=device, device_id_type=MESH)

    greet(other)
    for exists, device in (
        (has_prev_y, prev_y), (has_next_y, next_y), (has_prev_z, prev_z), (has_next_z, next_z),
    ):
        pl.when(exists)(functools.partial(greet, device))

    def planes(ref, field, first, count):
        return ref.at[field, pl.ds(first * rows, count * rows), :]

    def interior(ref, field):
        return planes(ref, field, EDGE, depth)

    def plane(p):
        return pl.ds(pl.multiple_of(p * rows, 8), rows)

    loads = []

    def load(src, dst):
        copy = pltpu.make_async_copy(src, dst, in_sem.at[len(loads)])
        copy.start()
        loads.append(copy)
        return copy

    stress_load = {f: load(str_hbm.at[f], interior(s0, f)) for f in (1, 3, 4, 2, 5, 0)}
    buoy_load = load(buoy_hbm, buoy)
    vel_load = load(vel_hbm, vin)
    lam_load = load(lam_hbm, lam)
    mu_load = load(mu_hbm, mu)
    peak_load = load(peak_hbm, peak_ref)

    for ref, fields in ((s0, (2, 4, 5)), (s1, (2, 4, 5)), (v1, (0, 1, 2)), (v2, (0, 1, 2))):
        for f in fields:
            for first in (0, EDGE + depth):
                ref[f, pl.ds(first * rows, EDGE * rows), :] = jnp.zeros((EDGE * rows, lanes), F32)

    def clear_recv(way, *refs):
        for ref in refs:
            for e in range(2 * STEPS):
                ref[e, way] = jnp.zeros(ref.shape[2:], ref.dtype)

    for exists, way, refs_of in (
        (has_prev_y, 0, (ywhole_recv, ypart_recv)),
        (has_next_y, 1, (ywhole_recv, ypart_recv)),
        (has_prev_z, 0, (zwhole_recv, zpart_recv)),
        (has_next_z, 1, (zwhole_recv, zpart_recv)),
    ):
        pl.when(jnp.logical_not(exists))(functools.partial(clear_recv, way, *refs_of))

    def clear_coef(way):
        coef_recv[way] = jnp.zeros(coef_recv.shape[1:], F32)

    pl.when(jnp.logical_not(has_prev_y))(functools.partial(clear_coef, 0))
    pl.when(jnp.logical_not(has_next_y))(functools.partial(clear_coef, 1))

    def set_damping():
        choice = prof_ref[0, 0, 0]
        peak = jnp.float32(0.0)
        for i in range(peak_ref.shape[0]):
            peak = peak + jnp.where(choice == i, peak_ref[i], 0.0)
        rate = flag_ref[0, 0, 0].astype(F32) * peak
        z = (lax.broadcasted_iota(jnp.int32, (depth, 8, lanes), 0) + gy * depth).astype(F32)
        q = (z + 0.5) / (depth * n_gy)
        damping = rate * (0.5 + 0.5 * q * q)
        divide = 1.0 + HALF * damping
        keep_ref[...] = (1.0 - HALF * damping) / divide
        gain_ref[...] = (NEAR * TIME_STEP) / divide

    slot = lax.broadcasted_iota(jnp.int32, (8, lanes), 0)
    lane = lax.broadcasted_iota(jnp.int32, (8, lanes), 1)
    near_lane = jnp.where(grp == 0, lanes - 1, 0)
    far_lane = jnp.where(grp == 0, lanes - 2, 1)

    def picker(k):
        hit = ((slot == 2 * k) & (lane == near_lane)) | ((slot == 2 * k + 1) & (lane == far_lane))
        return jnp.where(hit, 1.0, 0.0).astype(BF16)

    def placer(k, forward):
        near, far = slot == 2 * k, slot == 2 * k + 1
        if forward:
            one = (near & (lane == lanes - 1)) & (grp == 0)
            after = ((near & (lane == lanes - 2)) | (far & (lane == lanes - 1))) & (grp == 0)
            before = (near & (lane == 0)) & (grp == 1)
            whole = jnp.where(one, 1.0, 0.0)
        else:
            one = (near & (lane == 0)) & (grp == 1)
            after = (near & (lane == lanes - 1)) & (grp == 0)
            before = ((near & (lane == 1)) | (far & (lane == 0))) & (grp == 1)
            whole = jnp.where(one, -1.0, 0.0)
        return whole + jnp.where(after, RATIO, jnp.where(before, -RATIO, 0.0))

    def placer_of(kind):
        total = sum(pltpu.roll(placer(k, forward), lanes - 2 * k, 1) if k else placer(k, forward)
                    for k, (_, forward) in enumerate(kind["x"]))
        high = total.astype(BF16)
        return jnp.concatenate([high, (total - high.astype(F32)).astype(BF16)], axis=0)

    def send_columns(e, kind, ref):
        total = None
        for k, (f, _) in enumerate(kind["x"]):
            cells = ref[f, pl.ds(EDGE * rows, depth * rows), :]
            term = lax.dot_general(
                picker(k), cells.astype(BF16), (((1,), (1,)), ((), ())), preferred_element_type=F32
            )
            total = term if total is None else total + term
        grp_send[e] = total.astype(BF16)

    def columns_copy(e):
        return pltpu.make_async_remote_copy(
            src_ref=grp_send.at[e], dst_ref=grp_recv.at[e], send_sem=gsend_sem.at[e], recv_sem=grecv_sem.at[e],
            device_id=other, device_id_type=MESH,
        )

    def column_terms(e):
        got = grp_recv[e]
        pair = jnp.concatenate([got, got], axis=0)
        total = lax.dot_general(
            pair, placer_of(kinds[e]), (((0,), (0,)), ((), ())), preferred_element_type=F32
        )
        at = lax.broadcasted_iota(jnp.int32, total.shape, 1)
        edge = (at >= lanes - 2) == (grp == 0)
        edge = edge & ((at >= lanes - 2) | (at < 2))
        return [jnp.where(edge, pltpu.roll(total, 2 * k, 1) if k else total, 0.0) for k in range(3)]

    def row_at(ref, field, y):
        return ref.at[field, pl.ds(EDGE * rows + y, depth, stride=rows), :]

    def cell_row(ref, y):
        return ref.at[pl.ds(y, depth, stride=rows), :]

    kinds = (STRESS, MOTION) * STEPS
    refs = (s0, v1, s1, v2)
    axes = {
        "y": (
            ywhole_send, ywhole_recv, ypart_send, ypart_recv, ysend_sem, yrecv_sem,
            has_prev_y, has_next_y, prev_y, next_y,
        ),
        "z": (
            zwhole_send, zwhole_recv, zpart_send, zpart_recv, zsend_sem, zrecv_sem,
            has_prev_z, has_next_z, prev_z, next_z,
        ),
    }

    def face_copies(e, axis, upward):
        whole, whole_to, part, part_to, send_sem, recv_sem, _, _, before, after = axes[axis]
        way = 0 if upward else 1
        count = len(whole_list(kinds[e][axis], upward))
        return [
            pltpu.make_async_remote_copy(
                src_ref=src, dst_ref=dst, send_sem=send_sem.at[e, way, i], recv_sem=recv_sem.at[e, way, i],
                device_id=after if upward else before, device_id_type=MESH,
            )
            for i, (src, dst) in enumerate((
                (whole.at[e, way, pl.ds(0, count)], whole_to.at[e, way, pl.ds(0, count)]),
                (part.at[e, way], part_to.at[e, way]),
            ))
        ]

    def each_copy(e, axis, outgoing, act):
        has_before, has_after = axes[axis][6:8]
        for exists, upward in ((has_after, outgoing), (has_before, not outgoing)):
            @pl.when(exists)
            def _():
                for copy in face_copies(e, axis, upward):
                    act(copy)

    def start_faces(e, axis):
        each_copy(e, axis, True, lambda copy: copy.start())

    def wait_faces(e, axis):
        each_copy(e, axis, False, lambda copy: copy.wait_recv())

    def fill_faces(e, axis, value):
        whole, _, part, _ = axes[axis][:4]
        fields = kinds[e][axis]
        for way, upward in ((0, True), (1, False)):
            last_index = (rows if axis == "y" else depth) - 1

            def layer(k, far):
                return value(fields[k][0], last_index - far if upward else far)

            for place, k in enumerate(whole_list(fields, upward)):
                whole[e, way, place] = layer(k, 0)
            for k, (_, forward) in enumerate(fields):
                part[e, way, k] = layer(k, part_depth(forward, upward)).astype(BF16)

    def fill_rows(e):
        fill_faces(e, "y", lambda f, y: row_at(refs[e], f, y)[...])

    def fill_planes(e):
        fill_faces(e, "z", lambda f, z: refs[e][f, pl.ds((z + EDGE) * rows, rows), :])

    def material_row(k, stress, y):
        if not stress:
            return cell_row(buoy, y)[...]
        if k == 1:
            mu_row = cell_row(mu, y)[...]
            return cell_row(lam, y)[...] + (mu_row + mu_row)
        return cell_row(mu, y)[...]

    def fill_material():
        for way, (near, far) in ((0, (rows - 1, rows - 2)), (1, (0, 1))):
            coef_send[way, 0] = material_row(0, False, near)
            coef_send[way, 1] = material_row(0, False, far)
            coef_send[way, 2] = material_row(0, True, near)
            coef_send[way, 3] = material_row(1, True, near)
            coef_send[way, 4] = material_row(way, True, far)

    def material_copy(way):
        return pltpu.make_async_remote_copy(
            src_ref=coef_send.at[way], dst_ref=coef_recv.at[way],
            send_sem=csend_sem.at[way], recv_sem=crecv_sem.at[way],
            device_id=prev_y if way else next_y, device_id_type=MESH,
        )

    def completions(e):
        if e == 0:
            return {}
        missing = {}
        for way, upward in ((0, True), (1, False)):
            near, far = (0, 1) if upward else (rows - 1, rows - 2)
            sign = 1.0 if upward else -1.0

            def coef(k, layer):
                if kinds[e] is MOTION:
                    return coef_recv[way, layer]
                return coef_recv[way, 4 if layer else (3 if k == 1 else 2)]

            for k, (_, forward) in enumerate(kinds[e]["y"]):
                driver = kinds[e - 1]["y"][k][0]
                near_row = row_at(refs[e - 1], driver, near)[...]
                part = (sign * RATIO) * near_row
                if forward != upward:
                    far_row = row_at(refs[e - 1], driver, far)[...]
                    missing[way, k, 0] = coef(k, 0) * (sign * near_row + (sign * RATIO) * far_row)
                    missing[way, k, 1] = coef(k, 1) * part
                else:
                    missing[way, k, 0] = coef(k, 0) * part
        return missing

    def face_terms(e, axis, missing=None):
        _, whole, _, part = axes[axis][:4]
        fields = kinds[e][axis]
        terms = []
        for k, (_, forward) in enumerate(fields):
            layers = []
            for way, upward in ((0, True), (1, False)):
                got = [part[e, way, k].astype(F32)]
                if forward != upward:
                    got.insert(0, whole[e, way, whole_list(fields, upward).index(k)])
                if missing:
                    got = [layer + missing[way, k, i] for i, layer in enumerate(got)]
                layers.append(got)
            terms.append(halo_terms(forward, *layers, rows if axis == "y" else depth))
        return terms

    lane_id = lax.broadcasted_iota(jnp.int32, (rows, lanes), 1)
    row_id = lax.broadcasted_iota(jnp.int32, (rows, lanes), 0)

    def along_x(ref, field, p, forward):
        cells = ref[field, plane(p), :]
        one_back = jnp.where(lane_id >= 1, pltpu.roll(cells, 1, 1), 0.0)
        one_on = jnp.where(lane_id < lanes - 1, pltpu.roll(cells, lanes - 1, 1), 0.0)
        if forward:
            two_on = jnp.where(lane_id < lanes - 2, pltpu.roll(cells, lanes - 2, 1), 0.0)
            return one_on - cells, two_on - one_back
        two_back = jnp.where(lane_id >= 2, pltpu.roll(cells, 2, 1), 0.0)
        return cells - one_back, one_on - two_back

    def along_y(ref, field, p, forward):
        start = pl.multiple_of(p * rows, 8)

        def at(d):
            cells = ref[field, pl.ds(start + d, rows), :]
            if d == 0:
                return cells
            inside = row_id >= -d if d < 0 else row_id < rows - d
            return jnp.where(inside, cells, 0.0)

        if forward:
            return at(1) - at(0), at(2) - at(-1)
        return at(0) - at(-1), at(1) - at(-2)

    def along_z(ref, field, p, forward):
        at = lambda d: ref[field, plane(p + d), :]
        if forward:
            return at(1) - at(0), at(2) - at(-1)
        return at(0) - at(-1), at(1) - at(-2)

    def per_plane(ref, z):
        block = ref[z]
        return jnp.concatenate([block] * (rows // 8), axis=0)

    def inner(ref, z):
        return ref[plane(z), :]

    def joined(*parts):
        near = functools.reduce(lambda a, b: a + b, [n for n, _ in parts])
        far = functools.reduce(lambda a, b: a + b, [f for _, f in parts])
        return near + RATIO * far

    def motion_plane(src, old, new, z):
        p = z + EDGE
        keep, weight = per_plane(keep_ref, z), inner(buoy, z)
        cases = (
            ((along_x, 0, True), (along_y, 1, False), (along_z, 2, False)),
            ((along_x, 1, False), (along_y, 3, True), (along_z, 4, False)),
            ((along_x, 2, False), (along_y, 4, False), (along_z, 5, True)),
        )
        for k, case in enumerate(cases):
            force = joined(*[way(src, f, p, fwd) for way, f, fwd in case])
            new[k, plane(p), :] = keep * old(k, z) + weight * force

    def tensor_plane(src, old, store, z):
        p = z + EDGE
        keep, lam_z, mu_z = per_plane(keep_ref, z), inner(lam, z), inner(mu, z)
        xx = joined(along_x(src, 0, p, False))
        yy = joined(along_y(src, 1, p, False))
        zz = joined(along_z(src, 2, p, False))
        xy = joined(along_y(src, 0, p, True), along_x(src, 1, p, True))
        xz = joined(along_z(src, 0, p, True), along_x(src, 2, p, True))
        yz = joined(along_z(src, 1, p, True), along_y(src, 2, p, True))
        spread = lam_z * (xx + yy + zz)
        twice = mu_z + mu_z
        store(0, z, keep * old(0, z) + (spread + twice * xx))
        store(1, z, keep * old(1, z) + mu_z * xy)
        store(2, z, keep * old(2, z) + mu_z * xz)
        store(3, z, keep * old(3, z) + (spread + twice * yy))
        store(4, z, keep * old(4, z) + mu_z * yz)
        store(5, z, keep * old(5, z) + (spread + twice * zz))
        for f, value in enumerate((xx, xy, xz, yy, yz, zz)):
            strain[f, plane(z), :] = value

    def planes_loop(body):
        def step(z, carry):
            body(z)
            return carry

        lax.fori_loop(0, depth, step, 0, unroll=2)

    for f in (1, 3, 4):
        stress_load[f].wait()
    fill_rows(0)
    for f in (2, 5):
        stress_load[f].wait()
    fill_planes(0)
    stress_load[0].wait()

    neighbours = 1 + sum(e.astype(jnp.int32) for e in (has_prev_y, has_next_y, has_prev_z, has_next_z))
    pl.semaphore_wait(barrier, neighbours)
    start_faces(0, "y")
    start_faces(0, "z")
    send_columns(0, STRESS, s0)
    columns_copy(0).start()

    for copy in (peak_load, buoy_load, vel_load, lam_load, mu_load):
        copy.wait()
    set_damping()

    def scale(z):
        gain = per_plane(gain_ref, z)
        for ref in (buoy, lam, mu):
            ref[plane(z), :] = gain * ref[plane(z), :]

    planes_loop(scale)
    fill_material()

    def old_motion(ref):
        if ref is vin:
            return lambda k, z: vin[k, plane(z), :]
        return lambda k, z: ref[k, plane(z + EDGE), :]

    for step in range(STEPS):
        last = step == STEPS - 1
        e = 2 * step
        src, old, new = (s0, vin, v1) if step == 0 else (s1, v1, v2)
        planes_loop(functools.partial(motion_plane, src, old_motion(old), new))
        if step == 0:
            pl.when(has_next_y)(lambda: material_copy(0).start())
            pl.when(has_prev_y)(lambda: material_copy(1).start())
        columns_copy(e).wait_recv()
        for k, term in enumerate(column_terms(e)):
            cells = interior(new, k)
            cells[...] = cells[...] + buoy[...] * term
        wait_faces(e, "z")
        for k, terms in enumerate(face_terms(e, "z")):
            for z, term in terms.items():
                cells = new.at[k, pl.ds((z + EDGE) * rows, rows), :]
                cells[...] = cells[...] + buoy[pl.ds(z * rows, rows), :] * term
        fill_rows(e + 1)
        start_faces(e + 1, "y")
        missing = completions(e)
        wait_faces(e, "y")
        for k, terms in enumerate(face_terms(e, "y", missing)):
            for y, term in terms.items():
                row_at(new, k, y)[...] = row_at(new, k, y)[...] + cell_row(buoy, y)[...] * term
        fill_planes(e + 1)
        start_faces(e + 1, "z")
        send_columns(e + 1, MOTION, new)
        columns_copy(e + 1).start()

        e = e + 1
        src, old = (v1, s0) if step == 0 else (v2, s1)

        def old_tensor(f, z, ref=old):
            return ref[f, plane(z + EDGE), :]

        def store(f, z, value):
            if last:
                sfin[f, plane(z), :] = value
            else:
                s1[f, plane(z + EDGE), :] = value

        def correct(component, term, stress_at, cell_at, strain_at):
            changed = {}
            place = strain_at(component)
            place[...] = place[...] + term
            shear = cell_at(mu)[...] * term
            if component in NORMAL:
                spread = cell_at(lam)[...] * term
                for f in NORMAL:
                    changed[f] = spread + (shear + shear) if f == component else spread
            else:
                changed[component] = shear
            for f, amount in changed.items():
                changed[f] = stress_at(f)[...] + amount
                stress_at(f)[...] = changed[f]
            return changed

        def convert(components):
            def body(z):
                for f in components:
                    factor = NEAR if f in NORMAL else 0.5 * NEAR
                    eout[6 * step + f, plane(z), :] = (factor * strain[f, plane(z), :]).astype(BF16)

            planes_loop(body)

        planes_loop(functools.partial(tensor_plane, src, old_tensor, store))
        columns_copy(e).wait_recv()
        for k, term in enumerate(column_terms(e)):
            correct(
                STRAIN["x"][k], term,
                lambda f: sfin.at[f] if last else interior(s1, f),
                lambda ref: ref,
                lambda f: strain.at[f],
            )
        wait_faces(e, "z")
        for k, terms in enumerate(face_terms(e, "z")):
            for z, term in terms.items():
                cell = pl.ds(z * rows, rows)
                correct(
                    STRAIN["z"][k], term,
                    lambda f: sfin.at[f, cell, :] if last else s1.at[f, pl.ds((z + EDGE) * rows, rows), :],
                    lambda ref: ref.at[cell, :],
                    lambda f: strain.at[f, cell, :],
                )
        if last:
            convert((0, 2, 5))
        else:
            fill_rows(e + 1)
            start_faces(e + 1, "y")
        if e == 1:
            pl.when(has_prev_y)(lambda: material_copy(0).wait_recv())
            pl.when(has_next_y)(lambda: material_copy(1).wait_recv())
        missing = completions(e)
        wait_faces(e, "y")

        def stress_row(f, y):
            return cell_row(sfin.at[f], y) if last else row_at(s1, f, y)

        def change(f, y, amount):
            got = stress_row(f, y)[...] + amount
            stress_row(f, y)[...] = got
            return got

        shear_xy, normal_y, shear_yz = face_terms(e, "y", missing)
        spread = {y: cell_row(lam, y)[...] * term for y, term in normal_y.items()}
        for y, term in shear_yz.items():
            change(4, y, cell_row(mu, y)[...] * term)
        for y, amount in spread.items():
            change(5, y, amount)
        if not last:
            fill_planes(e + 1)
            start_faces(e + 1, "z")
        for y, amount in spread.items():
            change(0, y, amount)
        for y, term in shear_xy.items():
            change(1, y, cell_row(mu, y)[...] * term)
        if not last:
            send_columns(e + 1, STRESS, s1)
            columns_copy(e + 1).start()
        for y, term in normal_y.items():
            mu_row = cell_row(mu, y)[...]
            change(3, y, spread[y] + (mu_row + mu_row) * term)
        for f, terms in ((1, shear_xy), (3, normal_y), (4, shear_yz)):
            for y, term in terms.items():
                place = cell_row(strain.at[f], y)
                place[...] = place[...] + term
        convert((1, 3, 4) if last else range(6))

    for e in range(2 * STEPS):
        columns_copy(e).wait_send()
        for axis in axes:
            each_copy(e, axis, True, lambda copy: copy.wait_send())
    pl.when(has_next_y)(lambda: material_copy(0).wait_send())
    pl.when(has_prev_y)(lambda: material_copy(1).wait_send())


def write_out(v2, sfin, eout, vout_hbm, sout_hbm, eout_hbm, sem):
    cells = vout_hbm.shape[1]
    edge = (v2.shape[1] - cells) // 2
    copies = []

    def put(src, dst):
        copies.append(pltpu.make_async_copy(src, dst, sem.at[len(copies)]))
        copies[-1].start()

    for f in range(6):
        put(sfin.at[f], sout_hbm.at[f])
    for f in range(3):
        put(v2.at[f, pl.ds(edge, cells), :], vout_hbm.at[f])
    for f in range(6 * STEPS):
        put(eout.at[f], eout_hbm.at[f])
    for copy in copies:
        copy.wait()


def on_device(velocity, stress, buoyancy, lame_lambda, shear_modulus, pml_flag, profile_index, damping_peak):
    _, depth, rows, lanes = velocity.shape
    exchanges = 2 * STEPS
    cells = depth * rows
    any_spec = pl.BlockSpec(memory_space=pl.ANY)
    vmem_spec = pl.BlockSpec(memory_space=pltpu.VMEM)
    dma = pltpu.SemaphoreType.DMA
    halo_cells = (depth + 2 * EDGE) * rows

    def fields(count):
        return pltpu.VMEM((count, halo_cells, lanes), F32)

    final = pl.pallas_call(
        functools.partial(kernel, depth, rows, lanes),
        out_shape=(
            jax.ShapeDtypeStruct((3, halo_cells, lanes), F32),
            jax.ShapeDtypeStruct((6, cells, lanes), F32),
            jax.ShapeDtypeStruct((6 * STEPS, cells, lanes), BF16),
        ),
        in_specs=[any_spec] * 6 + [pl.BlockSpec(memory_space=pltpu.SMEM)] * 2,
        out_specs=(vmem_spec,) * 3,
        scratch_shapes=[
            fields(6),
            fields(6),
            fields(3),
            pltpu.VMEM((3, cells, lanes), F32),
            pltpu.VMEM((cells, lanes), F32),
            pltpu.VMEM((cells, lanes), F32),
            pltpu.VMEM((cells, lanes), F32),
            pltpu.VMEM((depth, 8, lanes), F32),
            pltpu.VMEM((depth, 8, lanes), F32),
            pltpu.VMEM((6, cells, lanes), F32),
            pltpu.SMEM(damping_peak.shape, F32),
            *[pltpu.VMEM((exchanges, 2, 2, depth, lanes), F32)] * 2,
            *[pltpu.VMEM((exchanges, 2, 3, depth, lanes), BF16)] * 2,
            *[pltpu.VMEM((exchanges, 2, 2, rows, lanes), F32)] * 2,
            *[pltpu.VMEM((exchanges, 2, 3, rows, lanes), BF16)] * 2,
            *[pltpu.VMEM((2, 5, depth, lanes), F32)] * 2,
            *[pltpu.VMEM((exchanges, 8, cells), BF16)] * 2,
            dma((11,)),
            *[dma((exchanges, 2, 2))] * 4,
            *[dma((2,))] * 2,
            *[dma((exchanges,))] * 2,
        ],
        compiler_params=pltpu.CompilerParams(
            collective_id=0, has_side_effects=True, vmem_limit_bytes=VMEM_LIMIT
        ),
        name="two_steps",
    )(
        *[
            pltpu.with_memory_space_constraint(x, pltpu.HBM)
            for x in (
                velocity.reshape(3, cells, lanes),
                stress.reshape(6, cells, lanes),
                buoyancy.reshape(cells, lanes),
                lame_lambda.reshape(cells, lanes),
                shear_modulus.reshape(cells, lanes),
                damping_peak,
            )
        ],
        pml_flag,
        profile_index,
    )
    vout, sout, eout = pl.pallas_call(
        write_out,
        out_shape=(
            jax.ShapeDtypeStruct((3, cells, lanes), F32),
            jax.ShapeDtypeStruct((6, cells, lanes), F32),
            jax.ShapeDtypeStruct((6 * STEPS, cells, lanes), BF16),
        ),
        in_specs=[any_spec] * 3,
        out_specs=(any_spec,) * 3,
        scratch_shapes=[dma((9 + 6 * STEPS,))],
        compiler_params=pltpu.CompilerParams(vmem_limit_bytes=VMEM_LIMIT),
        name="write_out",
    )(*final)
    return (
        vout.reshape(velocity.shape),
        sout.reshape(stress.shape),
        eout.reshape(STEPS, *stress.shape),
    )


def solution(mesh):
    return jax.shard_map(
        on_device,
        mesh=mesh,
        in_specs=(
            P(None, "gy", "gx", "grp"),
            P(None, "gy", "gx", "grp"),
            P("gy", "gx", "grp"),
            P("gy", "gx", "grp"),
            P("gy", "gx", "grp"),
            P("gy", "gx", "grp"),
            P("gy", "gx", "grp"),
            P(),
        ),
        out_specs=(
            P(None, "gy", "gx", "grp"),
            P(None, "gy", "gx", "grp"),
            P(None, None, "gy", "gx", "grp"),
        ),
        check_vma=False,
    )
```

```python
import functools

import jax
import jax.numpy as jnp
from jax import lax
from jax.experimental import pallas as pl
from jax.experimental.pallas import tpu as pltpu
from jax.sharding import PartitionSpec as P

MESH = pl.DeviceIdType.MESH
F32 = jnp.float32
BF16 = jnp.bfloat16

STEPS = 2
NEAR = 9.0 / 8.0
RATIO = -1.0 / 27.0
TIME_STEP = 0.15
HALF = 0.5 * TIME_STEP

EDGE = 2

VMEM_LIMIT = 24 * 1024 * 1024

STRESS = {
    "x": ((0, True), (1, False), (2, False)),
    "y": ((1, False), (3, True), (4, False)),
    "z": ((2, False), (4, False), (5, True)),
}
MOTION = {
    "x": ((0, False), (1, True), (2, True)),
    "y": ((0, True), (1, False), (2, True)),
    "z": ((0, True), (1, True), (2, False)),
}


STRAIN = {"x": (0, 1, 2), "y": (1, 3, 4), "z": (2, 4, 5)}
NORMAL = (0, 3, 5)


def whole_list(fields, upward):
    return [k for k, (_, forward) in enumerate(fields) if forward != upward]


def part_depth(forward, upward):
    return 1 if forward != upward else 0


def halo_terms(forward, before, after, length):
    if forward:
        return {
            0: -RATIO * before[0],
            length - 1: after[0] + RATIO * after[1],
            length - 2: RATIO * after[0],
        }
    return {
        0: -before[0] - RATIO * before[1],
        1: -RATIO * before[0],
        length - 1: RATIO * after[0],
    }


def kernel(
    depth, rows, lanes,
    vel_hbm, str_hbm, buoy_hbm, lam_hbm, mu_hbm, peak_hbm, flag_ref, prof_ref,
    v2, sfin, eout,
    s0, s1, v1, vin, buoy, lam, mu, keep_ref, gain_ref, strain, peak_ref,
    ywhole_send, ywhole_recv, ypart_send, ypart_recv, zwhole_send, zwhole_recv, zpart_send, zpart_recv,
    coef_send, coef_recv, grp_send, grp_recv,
    in_sem, ysend_sem, yrecv_sem, zsend_sem, zrecv_sem, csend_sem, crecv_sem, gsend_sem, grecv_sem,
):
    gx, gy, grp = lax.axis_index("gx"), lax.axis_index("gy"), lax.axis_index("grp")
    n_gx, n_gy = lax.axis_size("gx"), lax.axis_size("gy")
    has_prev_y, has_next_y = gx > 0, gx < n_gx - 1
    has_prev_z, has_next_z = gy > 0, gy < n_gy - 1
    prev_y, next_y = {"gx": gx - 1}, {"gx": gx + 1}
    prev_z, next_z = {"gy": gy - 1}, {"gy": gy + 1}
    other = {"grp": 1 - grp}

    barrier = pltpu.get_barrier_semaphore()

    def greet(device):
        pl.semaphore_signal(barrier, inc=1, device_id=device, device_id_type=MESH)

    greet(other)
    for exists, device in (
        (has_prev_y, prev_y), (has_next_y, next_y), (has_prev_z, prev_z), (has_next_z, next_z),
    ):
        pl.when(exists)(functools.partial(greet, device))

    def planes(ref, field, first, count):
        return ref.at[field, pl.ds(first * rows, count * rows), :]

    def interior(ref, field):
        return planes(ref, field, EDGE, depth)

    def plane(p):
        return pl.ds(pl.multiple_of(p * rows, 8), rows)

    loads = []

    def load(src, dst):
        copy = pltpu.make_async_copy(src, dst, in_sem.at[len(loads)])
        copy.start()
        loads.append(copy)
        return copy

    stress_load = {f: load(str_hbm.at[f], interior(s0, f)) for f in (1, 3, 4, 2, 5, 0)}
    buoy_load = load(buoy_hbm, buoy)
    vel_load = load(vel_hbm, vin)
    lam_load = load(lam_hbm, lam)
    mu_load = load(mu_hbm, mu)
    peak_load = load(peak_hbm, peak_ref)

    for ref, fields in ((s0, (2, 4, 5)), (s1, (2, 4, 5)), (v1, (0, 1, 2)), (v2, (0, 1, 2))):
        for f in fields:
            for first in (0, EDGE + depth):
                ref[f, pl.ds(first * rows, EDGE * rows), :] = jnp.zeros((EDGE * rows, lanes), F32)

    def clear_recv(way, *refs):
        for ref in refs:
            for e in range(2 * STEPS):
                ref[e, way] = jnp.zeros(ref.shape[2:], ref.dtype)

    for exists, way, refs_of in (
        (has_prev_y, 0, (ywhole_recv, ypart_recv)),
        (has_next_y, 1, (ywhole_recv, ypart_recv)),
        (has_prev_z, 0, (zwhole_recv, zpart_recv)),
        (has_next_z, 1, (zwhole_recv, zpart_recv)),
    ):
        pl.when(jnp.logical_not(exists))(functools.partial(clear_recv, way, *refs_of))

    def clear_coef(way):
        coef_recv[way] = jnp.zeros(coef_recv.shape[1:], F32)

    pl.when(jnp.logical_not(has_prev_y))(functools.partial(clear_coef, 0))
    pl.when(jnp.logical_not(has_next_y))(functools.partial(clear_coef, 1))

    def set_damping():
        choice = prof_ref[0, 0, 0]
        peak = jnp.float32(0.0)
        for i in range(peak_ref.shape[0]):
            peak = peak + jnp.where(choice == i, peak_ref[i], 0.0)
        rate = flag_ref[0, 0, 0].astype(F32) * peak
        z = (lax.broadcasted_iota(jnp.int32, (depth, 8, lanes), 0) + gy * depth).astype(F32)
        q = (z + 0.5) / (depth * n_gy)
        damping = rate * (0.5 + 0.5 * q * q)
        divide = 1.0 + HALF * damping
        keep_ref[...] = (1.0 - HALF * damping) / divide
        gain_ref[...] = (NEAR * TIME_STEP) / divide

    slot = lax.broadcasted_iota(jnp.int32, (8, lanes), 0)
    lane = lax.broadcasted_iota(jnp.int32, (8, lanes), 1)
    near_lane = jnp.where(grp == 0, lanes - 1, 0)
    far_lane = jnp.where(grp == 0, lanes - 2, 1)

    def picker(k):
        hit = ((slot == 2 * k) & (lane == near_lane)) | ((slot == 2 * k + 1) & (lane == far_lane))
        return jnp.where(hit, 1.0, 0.0).astype(BF16)

    def placer(k, forward):
        near, far = slot == 2 * k, slot == 2 * k + 1
        if forward:
            one = (near & (lane == lanes - 1)) & (grp == 0)
            after = ((near & (lane == lanes - 2)) | (far & (lane == lanes - 1))) & (grp == 0)
            before = (near & (lane == 0)) & (grp == 1)
            whole = jnp.where(one, 1.0, 0.0)
        else:
            one = (near & (lane == 0)) & (grp == 1)
            after = (near & (lane == lanes - 1)) & (grp == 0)
            before = ((near & (lane == 1)) | (far & (lane == 0))) & (grp == 1)
            whole = jnp.where(one, -1.0, 0.0)
        return whole + jnp.where(after, RATIO, jnp.where(before, -RATIO, 0.0))

    def placer_of(kind):
        total = sum(pltpu.roll(placer(k, forward), lanes - 2 * k, 1) if k else placer(k, forward)
                    for k, (_, forward) in enumerate(kind["x"]))
        high = total.astype(BF16)
        return jnp.concatenate([high, (total - high.astype(F32)).astype(BF16)], axis=0)

    def send_columns(e, kind, ref):
        total = None
        for k, (f, _) in enumerate(kind["x"]):
            cells = ref[f, pl.ds(EDGE * rows, depth * rows), :]
            term = lax.dot_general(
                picker(k), cells.astype(BF16), (((1,), (1,)), ((), ())), preferred_element_type=F32
            )
            total = term if total is None else total + term
        grp_send[e] = total.astype(BF16)

    def columns_copy(e):
        return pltpu.make_async_remote_copy(
            src_ref=grp_send.at[e], dst_ref=grp_recv.at[e], send_sem=gsend_sem.at[e], recv_sem=grecv_sem.at[e],
            device_id=other, device_id_type=MESH,
        )

    def column_terms(e):
        got = grp_recv[e]
        pair = jnp.concatenate([got, got], axis=0)
        total = lax.dot_general(
            pair, placer_of(kinds[e]), (((0,), (0,)), ((), ())), preferred_element_type=F32
        )
        at = lax.broadcasted_iota(jnp.int32, total.shape, 1)
        edge = (at >= lanes - 2) == (grp == 0)
        edge = edge & ((at >= lanes - 2) | (at < 2))
        return [jnp.where(edge, pltpu.roll(total, 2 * k, 1) if k else total, 0.0) for k in range(3)]

    def row_at(ref, field, y):
        return ref.at[field, pl.ds(EDGE * rows + y, depth, stride=rows), :]

    def cell_row(ref, y):
        return ref.at[pl.ds(y, depth, stride=rows), :]

    kinds = (STRESS, MOTION) * STEPS
    refs = (s0, v1, s1, v2)
    axes = {
        "y": (
            ywhole_send, ywhole_recv, ypart_send, ypart_recv, ysend_sem, yrecv_sem,
            has_prev_y, has_next_y, prev_y, next_y,
        ),
        "z": (
            zwhole_send, zwhole_recv, zpart_send, zpart_recv, zsend_sem, zrecv_sem,
            has_prev_z, has_next_z, prev_z, next_z,
        ),
    }

    def face_copies(e, axis, upward):
        whole, whole_to, part, part_to, send_sem, recv_sem, _, _, before, after = axes[axis]
        way = 0 if upward else 1
        count = len(whole_list(kinds[e][axis], upward))
        return [
            pltpu.make_async_remote_copy(
                src_ref=src, dst_ref=dst, send_sem=send_sem.at[e, way, i], recv_sem=recv_sem.at[e, way, i],
                device_id=after if upward else before, device_id_type=MESH,
            )
            for i, (src, dst) in enumerate((
                (whole.at[e, way, pl.ds(0, count)], whole_to.at[e, way, pl.ds(0, count)]),
                (part.at[e, way], part_to.at[e, way]),
            ))
        ]

    def each_copy(e, axis, outgoing, act):
        has_before, has_after = axes[axis][6:8]
        for exists, upward in ((has_after, outgoing), (has_before, not outgoing)):
            @pl.when(exists)
            def _():
                for copy in face_copies(e, axis, upward):
                    act(copy)

    def start_faces(e, axis):
        each_copy(e, axis, True, lambda copy: copy.start())

    def wait_faces(e, axis):
        each_copy(e, axis, False, lambda copy: copy.wait_recv())

    def fill_faces(e, axis, value):
        whole, _, part, _ = axes[axis][:4]
        fields = kinds[e][axis]
        for way, upward in ((0, True), (1, False)):
            last_index = (rows if axis == "y" else depth) - 1

            def layer(k, far):
                return value(fields[k][0], last_index - far if upward else far)

            for place, k in enumerate(whole_list(fields, upward)):
                whole[e, way, place] = layer(k, 0)
            for k, (_, forward) in enumerate(fields):
                part[e, way, k] = layer(k, part_depth(forward, upward)).astype(BF16)

    def fill_rows(e):
        fill_faces(e, "y", lambda f, y: row_at(refs[e], f, y)[...])

    def fill_planes(e):
        fill_faces(e, "z", lambda f, z: refs[e][f, pl.ds((z + EDGE) * rows, rows), :])

    def material_row(k, stress, y):
        if not stress:
            return cell_row(buoy, y)[...]
        if k == 1:
            mu_row = cell_row(mu, y)[...]
            return cell_row(lam, y)[...] + (mu_row + mu_row)
        return cell_row(mu, y)[...]

    def fill_material():
        for way, (near, far) in ((0, (rows - 1, rows - 2)), (1, (0, 1))):
            coef_send[way, 0] = material_row(0, False, near)
            coef_send[way, 1] = material_row(0, False, far)
            coef_send[way, 2] = material_row(0, True, near)
            coef_send[way, 3] = material_row(1, True, near)
            coef_send[way, 4] = material_row(way, True, far)

    def material_copy(way):
        return pltpu.make_async_remote_copy(
            src_ref=coef_send.at[way], dst_ref=coef_recv.at[way],
            send_sem=csend_sem.at[way], recv_sem=crecv_sem.at[way],
            device_id=prev_y if way else next_y, device_id_type=MESH,
        )

    def completions(e):
        if e == 0:
            return {}
        missing = {}
        for way, upward in ((0, True), (1, False)):
            near, far = (0, 1) if upward else (rows - 1, rows - 2)
            sign = 1.0 if upward else -1.0

            def coef(k, layer):
                if kinds[e] is MOTION:
                    return coef_recv[way, layer]
                return coef_recv[way, 4 if layer else (3 if k == 1 else 2)]

            for k, (_, forward) in enumerate(kinds[e]["y"]):
                driver = kinds[e - 1]["y"][k][0]
                near_row = row_at(refs[e - 1], driver, near)[...]
                part = (sign * RATIO) * near_row
                if forward != upward:
                    far_row = row_at(refs[e - 1], driver, far)[...]
                    missing[way, k, 0] = coef(k, 0) * (sign * near_row + (sign * RATIO) * far_row)
                    missing[way, k, 1] = coef(k, 1) * part
                else:
                    missing[way, k, 0] = coef(k, 0) * part
        return missing

    def face_terms(e, axis, missing=None):
        _, whole, _, part = axes[axis][:4]
        fields = kinds[e][axis]
        terms = []
        for k, (_, forward) in enumerate(fields):
            layers = []
            for way, upward in ((0, True), (1, False)):
                got = [part[e, way, k].astype(F32)]
                if forward != upward:
                    got.insert(0, whole[e, way, whole_list(fields, upward).index(k)])
                if missing:
                    got = [layer + missing[way, k, i] for i, layer in enumerate(got)]
                layers.append(got)
            terms.append(halo_terms(forward, *layers, rows if axis == "y" else depth))
        return terms

    lane_id = lax.broadcasted_iota(jnp.int32, (rows, lanes), 1)
    row_id = lax.broadcasted_iota(jnp.int32, (rows, lanes), 0)

    def along_x(ref, field, p, forward):
        cells = ref[field, plane(p), :]
        one_back = jnp.where(lane_id >= 1, pltpu.roll(cells, 1, 1), 0.0)
        one_on = jnp.where(lane_id < lanes - 1, pltpu.roll(cells, lanes - 1, 1), 0.0)
        if forward:
            two_on = jnp.where(lane_id < lanes - 2, pltpu.roll(cells, lanes - 2, 1), 0.0)
            return one_on - cells, two_on - one_back
        two_back = jnp.where(lane_id >= 2, pltpu.roll(cells, 2, 1), 0.0)
        return cells - one_back, one_on - two_back

    def along_y(ref, field, p, forward):
        start = pl.multiple_of(p * rows, 8)

        def at(d):
            cells = ref[field, pl.ds(start + d, rows), :]
            if d == 0:
                return cells
            inside = row_id >= -d if d < 0 else row_id < rows - d
            return jnp.where(inside, cells, 0.0)

        if forward:
            return at(1) - at(0), at(2) - at(-1)
        return at(0) - at(-1), at(1) - at(-2)

    def along_z(ref, field, p, forward):
        at = lambda d: ref[field, plane(p + d), :]
        if forward:
            return at(1) - at(0), at(2) - at(-1)
        return at(0) - at(-1), at(1) - at(-2)

    def per_plane(ref, z):
        block = ref[z]
        return jnp.concatenate([block] * (rows // 8), axis=0)

    def inner(ref, z):
        return ref[plane(z), :]

    def joined(*parts):
        near = functools.reduce(lambda a, b: a + b, [n for n, _ in parts])
        far = functools.reduce(lambda a, b: a + b, [f for _, f in parts])
        return near + RATIO * far

    def motion_plane(src, old, new, z):
        p = z + EDGE
        keep, weight = per_plane(keep_ref, z), inner(buoy, z)
        cases = (
            ((along_x, 0, True), (along_y, 1, False), (along_z, 2, False)),
            ((along_x, 1, False), (along_y, 3, True), (along_z, 4, False)),
            ((along_x, 2, False), (along_y, 4, False), (along_z, 5, True)),
        )
        for k, case in enumerate(cases):
            force = joined(*[way(src, f, p, fwd) for way, f, fwd in case])
            new[k, plane(p), :] = keep * old(k, z) + weight * force

    def tensor_plane(src, old, store, z):
        p = z + EDGE
        keep, lam_z, mu_z = per_plane(keep_ref, z), inner(lam, z), inner(mu, z)
        xx = joined(along_x(src, 0, p, False))
        yy = joined(along_y(src, 1, p, False))
        zz = joined(along_z(src, 2, p, False))
        xy = joined(along_y(src, 0, p, True), along_x(src, 1, p, True))
        xz = joined(along_z(src, 0, p, True), along_x(src, 2, p, True))
        yz = joined(along_z(src, 1, p, True), along_y(src, 2, p, True))
        spread = lam_z * (xx + yy + zz)
        twice = mu_z + mu_z
        store(0, z, keep * old(0, z) + (spread + twice * xx))
        store(1, z, keep * old(1, z) + mu_z * xy)
        store(2, z, keep * old(2, z) + mu_z * xz)
        store(3, z, keep * old(3, z) + (spread + twice * yy))
        store(4, z, keep * old(4, z) + mu_z * yz)
        store(5, z, keep * old(5, z) + (spread + twice * zz))
        for f, value in enumerate((xx, xy, xz, yy, yz, zz)):
            strain[f, plane(z), :] = value

    def planes_loop(body):
        def step(z, carry):
            body(z)
            return carry

        lax.fori_loop(0, depth, step, 0)

    for f in (1, 3, 4):
        stress_load[f].wait()
    fill_rows(0)
    for f in (2, 5):
        stress_load[f].wait()
    fill_planes(0)
    stress_load[0].wait()

    neighbours = 1 + sum(e.astype(jnp.int32) for e in (has_prev_y, has_next_y, has_prev_z, has_next_z))
    pl.semaphore_wait(barrier, neighbours)
    start_faces(0, "y")
    start_faces(0, "z")
    send_columns(0, STRESS, s0)
    columns_copy(0).start()

    for copy in (peak_load, buoy_load, vel_load, lam_load, mu_load):
        copy.wait()
    set_damping()

    def scale(z):
        gain = per_plane(gain_ref, z)
        for ref in (buoy, lam, mu):
            ref[plane(z), :] = gain * ref[plane(z), :]

    planes_loop(scale)
    fill_material()

    def old_motion(ref):
        if ref is vin:
            return lambda k, z: vin[k, plane(z), :]
        return lambda k, z: ref[k, plane(z + EDGE), :]

    for step in range(STEPS):
        last = step == STEPS - 1
        e = 2 * step
        src, old, new = (s0, vin, v1) if step == 0 else (s1, v1, v2)
        planes_loop(functools.partial(motion_plane, src, old_motion(old), new))
        if step == 0:
            pl.when(has_next_y)(lambda: material_copy(0).start())
            pl.when(has_prev_y)(lambda: material_copy(1).start())
        columns_copy(e).wait_recv()
        for k, term in enumerate(column_terms(e)):
            cells = interior(new, k)
            cells[...] = cells[...] + buoy[...] * term
        wait_faces(e, "z")
        for k, terms in enumerate(face_terms(e, "z")):
            for z, term in terms.items():
                cells = new.at[k, pl.ds((z + EDGE) * rows, rows), :]
                cells[...] = cells[...] + buoy[pl.ds(z * rows, rows), :] * term
        fill_rows(e + 1)
        start_faces(e + 1, "y")
        missing = completions(e)
        wait_faces(e, "y")
        for k, terms in enumerate(face_terms(e, "y", missing)):
            for y, term in terms.items():
                row_at(new, k, y)[...] = row_at(new, k, y)[...] + cell_row(buoy, y)[...] * term
        fill_planes(e + 1)
        start_faces(e + 1, "z")
        send_columns(e + 1, MOTION, new)
        columns_copy(e + 1).start()

        e = e + 1
        src, old = (v1, s0) if step == 0 else (v2, s1)

        def old_tensor(f, z, ref=old):
            return ref[f, plane(z + EDGE), :]

        def store(f, z, value):
            if last:
                sfin[f, plane(z), :] = value
            else:
                s1[f, plane(z + EDGE), :] = value

        def correct(component, term, stress_at, cell_at, strain_at):
            changed = {}
            place = strain_at(component)
            place[...] = place[...] + term
            shear = cell_at(mu)[...] * term
            if component in NORMAL:
                spread = cell_at(lam)[...] * term
                for f in NORMAL:
                    changed[f] = spread + (shear + shear) if f == component else spread
            else:
                changed[component] = shear
            for f, amount in changed.items():
                changed[f] = stress_at(f)[...] + amount
                stress_at(f)[...] = changed[f]
            return changed

        def convert(components):
            def body(z):
                for f in components:
                    factor = NEAR if f in NORMAL else 0.5 * NEAR
                    eout[6 * step + f, plane(z), :] = (factor * strain[f, plane(z), :]).astype(BF16)

            planes_loop(body)

        planes_loop(functools.partial(tensor_plane, src, old_tensor, store))
        columns_copy(e).wait_recv()
        for k, term in enumerate(column_terms(e)):
            correct(
                STRAIN["x"][k], term,
                lambda f: sfin.at[f] if last else interior(s1, f),
                lambda ref: ref,
                lambda f: strain.at[f],
            )
        wait_faces(e, "z")
        for k, terms in enumerate(face_terms(e, "z")):
            for z, term in terms.items():
                cell = pl.ds(z * rows, rows)
                correct(
                    STRAIN["z"][k], term,
                    lambda f: sfin.at[f, cell, :] if last else s1.at[f, pl.ds((z + EDGE) * rows, rows), :],
                    lambda ref: ref.at[cell, :],
                    lambda f: strain.at[f, cell, :],
                )
        if last:
            convert((0, 2, 5))
            for sent in range(2 * STEPS):
                columns_copy(sent).wait_send()
                for axis in axes:
                    each_copy(sent, axis, True, lambda copy: copy.wait_send())
            pl.when(has_next_y)(lambda: material_copy(0).wait_send())
            pl.when(has_prev_y)(lambda: material_copy(1).wait_send())
        else:
            fill_rows(e + 1)
            start_faces(e + 1, "y")
        if e == 1:
            pl.when(has_prev_y)(lambda: material_copy(0).wait_recv())
            pl.when(has_next_y)(lambda: material_copy(1).wait_recv())
        missing = completions(e)
        wait_faces(e, "y")

        def stress_row(f, y):
            return cell_row(sfin.at[f], y) if last else row_at(s1, f, y)

        def change(f, y, amount):
            got = stress_row(f, y)[...] + amount
            stress_row(f, y)[...] = got
            return got

        shear_xy, normal_y, shear_yz = face_terms(e, "y", missing)
        spread = {y: cell_row(lam, y)[...] * term for y, term in normal_y.items()}
        for y, term in shear_yz.items():
            change(4, y, cell_row(mu, y)[...] * term)
        for y, amount in spread.items():
            change(5, y, amount)
        if not last:
            fill_planes(e + 1)
            start_faces(e + 1, "z")
        for y, amount in spread.items():
            change(0, y, amount)
        for y, term in shear_xy.items():
            change(1, y, cell_row(mu, y)[...] * term)
        if not last:
            send_columns(e + 1, STRESS, s1)
            columns_copy(e + 1).start()
        for y, term in normal_y.items():
            mu_row = cell_row(mu, y)[...]
            change(3, y, spread[y] + (mu_row + mu_row) * term)
        for f, terms in ((1, shear_xy), (3, normal_y), (4, shear_yz)):
            for y, term in terms.items():
                place = cell_row(strain.at[f], y)
                place[...] = place[...] + term
        convert((1, 3, 4) if last else range(6))


def write_out(v2, sfin, eout, vout_hbm, sout_hbm, eout_hbm, sem):
    cells = vout_hbm.shape[1]
    edge = (v2.shape[1] - cells) // 2
    copies = []

    def put(src, dst):
        copies.append(pltpu.make_async_copy(src, dst, sem.at[len(copies)]))
        copies[-1].start()

    for f in range(6):
        put(sfin.at[f], sout_hbm.at[f])
    for f in range(3):
        put(v2.at[f, pl.ds(edge, cells), :], vout_hbm.at[f])
    for f in range(6 * STEPS):
        put(eout.at[f], eout_hbm.at[f])
    for copy in copies:
        copy.wait()


def on_device(velocity, stress, buoyancy, lame_lambda, shear_modulus, pml_flag, profile_index, damping_peak):
    _, depth, rows, lanes = velocity.shape
    exchanges = 2 * STEPS
    cells = depth * rows
    any_spec = pl.BlockSpec(memory_space=pl.ANY)
    vmem_spec = pl.BlockSpec(memory_space=pltpu.VMEM)
    dma = pltpu.SemaphoreType.DMA
    halo_cells = (depth + 2 * EDGE) * rows

    def fields(count):
        return pltpu.VMEM((count, halo_cells, lanes), F32)

    final = pl.pallas_call(
        functools.partial(kernel, depth, rows, lanes),
        out_shape=(
            jax.ShapeDtypeStruct((3, halo_cells, lanes), F32),
            jax.ShapeDtypeStruct((6, cells, lanes), F32),
            jax.ShapeDtypeStruct((6 * STEPS, cells, lanes), BF16),
        ),
        in_specs=[any_spec] * 6 + [pl.BlockSpec(memory_space=pltpu.SMEM)] * 2,
        out_specs=(vmem_spec,) * 3,
        scratch_shapes=[
            fields(6),
            fields(6),
            fields(3),
            pltpu.VMEM((3, cells, lanes), F32),
            pltpu.VMEM((cells, lanes), F32),
            pltpu.VMEM((cells, lanes), F32),
            pltpu.VMEM((cells, lanes), F32),
            pltpu.VMEM((depth, 8, lanes), F32),
            pltpu.VMEM((depth, 8, lanes), F32),
            pltpu.VMEM((6, cells, lanes), F32),
            pltpu.SMEM(damping_peak.shape, F32),
            *[pltpu.VMEM((exchanges, 2, 2, depth, lanes), F32)] * 2,
            *[pltpu.VMEM((exchanges, 2, 3, depth, lanes), BF16)] * 2,
            *[pltpu.VMEM((exchanges, 2, 2, rows, lanes), F32)] * 2,
            *[pltpu.VMEM((exchanges, 2, 3, rows, lanes), BF16)] * 2,
            *[pltpu.VMEM((2, 5, depth, lanes), F32)] * 2,
            *[pltpu.VMEM((exchanges, 8, cells), BF16)] * 2,
            dma((11,)),
            *[dma((exchanges, 2, 2))] * 4,
            *[dma((2,))] * 2,
            *[dma((exchanges,))] * 2,
        ],
        compiler_params=pltpu.CompilerParams(
            collective_id=0, has_side_effects=True, vmem_limit_bytes=VMEM_LIMIT
        ),
        name="two_steps",
    )(
        *[
            pltpu.with_memory_space_constraint(x, pltpu.HBM)
            for x in (
                velocity.reshape(3, cells, lanes),
                stress.reshape(6, cells, lanes),
                buoyancy.reshape(cells, lanes),
                lame_lambda.reshape(cells, lanes),
                shear_modulus.reshape(cells, lanes),
                damping_peak,
            )
        ],
        pml_flag,
        profile_index,
    )
    vout, sout, eout = pl.pallas_call(
        write_out,
        out_shape=(
            jax.ShapeDtypeStruct((3, cells, lanes), F32),
            jax.ShapeDtypeStruct((6, cells, lanes), F32),
            jax.ShapeDtypeStruct((6 * STEPS, cells, lanes), BF16),
        ),
        in_specs=[any_spec] * 3,
        out_specs=(any_spec,) * 3,
        scratch_shapes=[dma((9 + 6 * STEPS,))],
        compiler_params=pltpu.CompilerParams(vmem_limit_bytes=VMEM_LIMIT),
        name="write_out",
    )(*final)
    return (
        vout.reshape(velocity.shape),
        sout.reshape(stress.shape),
        eout.reshape(STEPS, *stress.shape),
    )


def solution(mesh):
    return jax.shard_map(
        on_device,
        mesh=mesh,
        in_specs=(
            P(None, "gy", "gx", "grp"),
            P(None, "gy", "gx", "grp"),
            P("gy", "gx", "grp"),
            P("gy", "gx", "grp"),
            P("gy", "gx", "grp"),
            P("gy", "gx", "grp"),
            P("gy", "gx", "grp"),
            P(),
        ),
        out_specs=(
            P(None, "gy", "gx", "grp"),
            P(None, "gy", "gx", "grp"),
            P(None, None, "gy", "gx", "grp"),
        ),
        check_vma=False,
    )
```
